128 devices in a mesh: occ: 4 (over x_lo, core), blk: 32 (over y, z, x_hi).
Axes of the slice: x: 4 (x_hi: 2, x_lo: 2; x = x_hi * 2 + x_lo), y: 4, z: 4, core: 2. Of those that a mesh axis runs over, the one named last changes fastest.
Arguments:
- half_rows: float32 [12, 4096, 3072], P(None, ('occ', 'blk')), may hold values from -6 to 6
- screen: int32 [12, 512], P(None, ('occ', 'blk')), may hold values 0 or 1
- slot_shell: int32 [512], replicated, may hold values from -1 to 143, as said below
- vir_coeff: float32 [1152, 1024], replicated, may hold values from -0.0234375 to 0.0234375
- occ_energy: float32 [12], P('occ'), may hold values from -2 to -0.3
- vir_energy: float32 [1024], P('blk'), may hold values from 0.1 to 3
- pair_list: int32 [24, 2], P('occ'), may hold values from 0 to 2, as said below
Outputs:
- gamma: float32 [12, 1024, 3072], P('occ', 'blk')
The draws below stay inside these ranges and needn't reach their ends.
Inputs may be any that keep to these rules, and one draw needn't show every extreme that they name: `slot_shell`: every shell block 0 to 143 stands in exactly one slot; -1 marks an empty slot; some owner has all 4 of its slots filled. `pair_list`: the 6 entries of each group are distinct ordered pairs.
All inputs are finite; a program needn't handle non-finite values. No bound on the sum of `screen` on one device may be relied on, other than what follows from the above.
Results may differ from the reference program's by a relative error of at most 0.0001.
Values sent between devices are 32-bit elements; how exact they have to be, the bound alone decides.
No kernel may reach another device: no remote copies, remote signals or barrier semaphores. Data moves between devices by JAX's collectives and lax.ppermute only.
A program may use at most 128 MiB of HBM per device.

```python
import math
import jax
import jax.numpy as jnp
from jax import lax

NVIR = 1024
NAUX = 3072
SHW = 8
NSH = 144
ACT = 3
PAIRS = 6
OWNERS = 128
SLOTS = 4
NACT = 12
NAO = 1152


def draw_slot_shell(key, part):
    key_full = jax.random.fold_in(key, 11)
    key_place = jax.random.fold_in(key, 12)
    key_order = jax.random.fold_in(key, 13)
    busiest = jax.random.randint(key_full, (), 0, OWNERS)
    others = NSH - SLOTS
    capacity = (OWNERS - 1) * SLOTS
    places = jax.random.permutation(key_place, capacity)[:others]
    shells = jax.random.permutation(key_order, NSH).astype(jnp.int32)
    device_ids = (busiest + 1 + places // SLOTS) % OWNERS
    positions = (device_ids * SLOTS + places % SLOTS).astype(jnp.int32)
    table = jnp.full((OWNERS * SLOTS,), -1, dtype=jnp.int32)
    first_slots = (busiest * SLOTS + jnp.arange(SLOTS)).astype(jnp.int32)
    table = table.at[first_slots].set(shells[:SLOTS])
    table = table.at[positions].set(shells[SLOTS:])
    return table


def draw_pair_list(key, part):
    groups = NACT // ACT
    keys = jax.random.split(jax.random.fold_in(key, 21), groups)
    picks = jax.vmap(lambda one_key: jax.random.permutation(one_key, ACT * ACT)[:PAIRS])(keys)
    picks = picks.reshape(-1).astype(jnp.int32)
    return jnp.stack([picks // ACT, picks % ACT], axis=1).astype(jnp.int32)


def plant(drawn, key, smallest, largest):
    longest = drawn.shape.index(max(drawn.shape))
    spots = []
    for shift in (0, 1):
        where = [jax.random.randint(jax.random.fold_in(key, axis), (), 0, length) for axis, length in enumerate(drawn.shape)]
        where[longest] = (where[longest] + shift) % drawn.shape[longest]
        spots.append(tuple(where))
    return drawn.at[spots[0]].set(smallest).at[spots[1]].set(largest)


def shard_levels(own_key, shape, cuts, smallest, top_value):
    factor_of = 1.0
    for position, parts in cuts:
        draws = jax.random.uniform(jax.random.fold_in(jax.random.fold_in(own_key, 6), position), (parts,), jnp.float32, smallest / len(cuts), top_value / len(cuts))
        factor_of = factor_of * jnp.repeat(jnp.exp(draws), shape[position] // parts).reshape((-1,) + (1,) * (len(shape) - 1 - position))
    return factor_of


def scatter_about(rng, extent, scale, most, shards=(), kind=jnp.bfloat16):
    values = jax.random.normal(rng, extent, jnp.float32) * scale
    if len(shards) > 0:
        values = shard_levels(rng, extent, shards, -0.22, 0.18) * values
    return jnp.clip(values, min=-most, max=most).astype(kind)


def setup_inputs(seed: int = 0) -> dict:
    streams_of = jax.random.split(jax.random.key(seed), 8)
    half_rows = scatter_about(streams_of[0], (NACT, OWNERS * SLOTS * SHW, NAUX), 1.0, 6.0, ((1, 128),), jnp.float32)
    screen = plant((jax.random.randint(streams_of[1], (NACT, OWNERS * SLOTS), 0, 4) < 3).astype(jnp.int32), jax.random.fold_in(streams_of[1], 1), 0, 1)
    slot_shell = draw_slot_shell(jax.random.fold_in(streams_of[7], 71), 0)
    vir_coeff = scatter_about(streams_of[3], (NAO, NVIR), (64 * NAO) ** -0.5, 0.0234375, (), jnp.float32)
    occ_energy = jnp.clip(-2.0 + 1.7 * jax.random.uniform(streams_of[4], (NACT,), jnp.float32) ** shard_levels(streams_of[4], (NACT,), ((0, 4),), -0.2, 0.2), -2.0, -0.3)
    vir_energy = jnp.clip(jnp.exp(math.log(3.0) - 3.4011974 * jax.random.uniform(streams_of[5], (NVIR,), jnp.float32) ** shard_levels(streams_of[5], (NVIR,), ((0, 32),), -0.2, 0.2)), 0.1, 3.0)
    pair_list = draw_pair_list(jax.random.fold_in(streams_of[7], 71), 0)
    return {"half_rows": half_rows, "screen": screen, "slot_shell": slot_shell, "vir_coeff": vir_coeff, "occ_energy": occ_energy, "vir_energy": vir_energy, "pair_list": pair_list}


def reference(half_rows, screen, slot_shell, vir_coeff, occ_energy, vir_energy, pair_list):
    orbitals = half_rows.shape[0]
    row_count = half_rows.shape[1]
    slot_total = slot_shell.shape[0]
    kept_rows = (half_rows.reshape(orbitals, slot_total, SHW, NAUX) * screen.astype(jnp.float32)[:, :, None, None]).reshape(orbitals, row_count, NAUX)
    blocks = vir_coeff.reshape(NSH, SHW, NVIR)[jnp.maximum(slot_shell, 0)]
    blocks = jnp.where((slot_shell >= 0)[:, None, None], blocks, jnp.zeros_like(blocks))
    coeff_rows = blocks.reshape(row_count, NVIR)
    fitted = jnp.einsum('irp,ra->iap', kept_rows, coeff_rows, precision=lax.Precision.HIGHEST)
    orbital_ids = jnp.arange(ACT, dtype=jnp.int32)
    results = []
    for group in range(orbitals // ACT):
        local = fitted[group * ACT:(group + 1) * ACT]
        energies = occ_energy[group * ACT:(group + 1) * ACT]
        listed = pair_list[group * PAIRS:(group + 1) * PAIRS]
        first = listed[:, 0][:, None, None] == orbital_ids[None, :, None]
        second = listed[:, 1][:, None, None] == orbital_ids[None, None, :]
        selected = jnp.sum((first & second).astype(jnp.float32), axis=0)
        coulomb = jnp.einsum('iap,jbp->iajb', local, local, precision=lax.Precision.HIGHEST)
        swapped = jnp.transpose(coulomb, (2, 1, 0, 3))
        denominator = energies[:, None, None, None] + energies[None, None, :, None] - vir_energy[None, :, None, None] - vir_energy[None, None, None, :]
        weight = selected[:, None, :, None] * ((2.0 * coulomb - swapped) / denominator)
        results.append(jnp.einsum('iajb,jbp->iap', weight, local, precision=lax.Precision.HIGHEST))
    return jnp.concatenate(results, axis=0)
```

```python
import jax
import jax.numpy as jnp
from jax import lax
from jax.experimental import pallas as pl
from jax.experimental.pallas import tpu as pltpu
from jax.sharding import Mesh, PartitionSpec as P

NVIR = 1024
SHW = 8
NSH = 144
ROWS = NSH * SHW
AUX = 3072
ALL = ("xl", "co", "y", "z", "xh")
GROUP = ("y", "z", "xh")
VLIM = 60 * 1024 * 1024
f32 = jnp.float32
bf16 = jnp.bfloat16


def params():
    return pltpu.CompilerParams(vmem_limit_bytes=VLIM)


def swap4(v):
    lane = lax.broadcasted_iota(jnp.int32, v[0].shape, 1)
    low = lane < 64
    even = (lane // 32) % 2 == 0
    a0 = jnp.where(low, v[0], pltpu.roll(v[2], 64, 1))
    a2 = jnp.where(low, pltpu.roll(v[0], 64, 1), v[2])
    a1 = jnp.where(low, v[1], pltpu.roll(v[3], 64, 1))
    a3 = jnp.where(low, pltpu.roll(v[1], 64, 1), v[3])
    w0 = jnp.where(even, a0, pltpu.roll(a1, 32, 1))
    w1 = jnp.where(even, pltpu.roll(a0, 96, 1), a1)
    w2 = jnp.where(even, a2, pltpu.roll(a3, 32, 1))
    w3 = jnp.where(even, pltpu.roll(a2, 96, 1), a3)
    return w0, w1, w2, w3


def split(x):
    hi = x.astype(bf16)
    lo = (x - hi.astype(f32)).astype(bf16)
    return hi, lo


def pack_kernel(scr_ref, x_ref, o_ref):
    for g in range(4):
        for s in range(4):
            for u in range(2):
                v = []
                for h in range(4):
                    i, t = divmod(4 * u + h, 3)
                    keep = scr_ref[3 * g + i, s].astype(f32)
                    v.append(x_ref[3 * g + i, 8 * s : 8 * s + 8, 128 * t : 128 * t + 128] * keep)
                w = swap4(v)
                for q in range(4):
                    o_ref[g, q, 8 * (2 * s + u) : 8 * (2 * s + u) + 8, :] = w[q]
        v = []
        for s in range(4):
            keep = scr_ref[3 * g + 2, s].astype(f32)
            v.append(x_ref[3 * g + 2, 8 * s : 8 * s + 8, 256:384] * keep)
        w = swap4(v)
        for q in range(4):
            o_ref[g, q, 64:72, :] = w[q]


def pack(half_rows, screen):
    return pl.pallas_call(
        pack_kernel,
        grid=(8,),
        in_specs=[
            pl.BlockSpec(memory_space=pltpu.SMEM),
            pl.BlockSpec((12, 32, 384), lambda m: (0, 0, m)),
        ],
        out_specs=pl.BlockSpec((4, 4, 72, 128), lambda m: (0, m, 0, 0)),
        out_shape=jax.ShapeDtypeStruct((4, 32, 72, 128), f32),
        compiler_params=params(),
        name="pack_rows",
    )(screen, half_rows)


def coeff_kernel(c_ref, hi_ref, lo_ref):
    hi, lo = split(c_ref[...].T)
    hi_ref[...] = hi
    lo_ref[...] = lo


def coeff(vir_coeff):
    return pl.pallas_call(
        coeff_kernel,
        grid=(9,),
        in_specs=[pl.BlockSpec((128, NVIR), lambda k: (k, 0))],
        out_specs=[pl.BlockSpec((NVIR, 128), lambda k: (0, k))] * 2,
        out_shape=[jax.ShapeDtypeStruct((NVIR, ROWS), bf16)] * 2,
        compiler_params=params(),
        name="split_coeff",
    )(vir_coeff)


def transform_kernel(inv_ref, r_ref, ve_ref, chi_ref, clo_ref, o_ref, xhi, xlo):
    @pl.when(pl.program_id(0) == 0)
    def _():
        def body(h, carry):
            tiles = []
            for e in range(2):
                where = inv_ref[2 * h + e]
                owner = where // 4
                slot = where % 4
                at = pl.multiple_of(slot * 16, 16)
                t01 = r_ref[owner, pl.ds(at, 16), :]
                t2 = pltpu.roll(r_ref[owner, 64:72, :], (128 - 32 * slot) % 128, 1)
                tiles.append((t01[:8], t01[8:], t2))
            row = pl.multiple_of(h * 16, 16)
            for n in range(3):
                hi, lo = split(jnp.concatenate([tiles[0][n], tiles[1][n]], axis=0))
                xhi[pl.ds(row, 16), 128 * n : 128 * n + 128] = hi
                xlo[pl.ds(row, 16), 128 * n : 128 * n + 128] = lo
            return carry

        lax.fori_loop(0, NSH // 2, body, 0, unroll=4)

    hi = chi_ref[...]
    y = jnp.dot(hi, xhi[...], preferred_element_type=f32)
    y += jnp.dot(hi, xlo[...], preferred_element_type=f32)
    y += jnp.dot(clo_ref[...], xhi[...], preferred_element_type=f32)
    lane = lax.broadcasted_iota(jnp.int32, (8, 128), 1) // 32
    for k in range(8):
        last = jnp.zeros((8, 128), f32)
        for ag in range(4):
            rows = slice(32 * k + 8 * ag, 32 * k + 8 * ag + 8)
            for u in range(2):
                o_ref[k, 8 * (2 * ag + u) : 8 * (2 * ag + u) + 8, :] = y[rows, 128 * u : 128 * u + 128]
            piece = y[rows, 256:384]
            if ag:
                piece = pltpu.roll(piece, 32 * ag, 1)
            last = jnp.where(lane == ag, piece, last)
        o_ref[k, 64:72, :] = last
        o_ref[k, 72:80, :] = jnp.broadcast_to(ve_ref[...], (8, 128))


def transform(inv, rows, energy_row, chi, clo):
    return pl.pallas_call(
        transform_kernel,
        grid=(4,),
        in_specs=[
            pl.BlockSpec(memory_space=pltpu.SMEM),
            pl.BlockSpec((128, 72, 128), lambda m: (0, 0, 0)),
            pl.BlockSpec((1, 128), lambda m: (0, 0)),
            pl.BlockSpec((256, ROWS), lambda m: (m, 0)),
            pl.BlockSpec((256, ROWS), lambda m: (m, 0)),
        ],
        out_specs=pl.BlockSpec((8, 80, 128), lambda m: (m, 0, 0)),
        out_shape=jax.ShapeDtypeStruct((32, 80, 128), f32),
        scratch_shapes=[pltpu.VMEM((ROWS, 384), bf16), pltpu.VMEM((ROWS, 384), bf16)],
        compiler_params=params(),
        name="transform_rows",
    )(inv, rows, energy_row, chi, clo)


def unpack_kernel(q_ref, f_ref, e_ref):
    def body(m, carry):
        for ag in range(4):
            for u in range(2):
                w = swap4([q_ref[4 * m + q, 8 * (2 * ag + u) : 8 * (2 * ag + u) + 8, :] for q in range(4)])
                for h in range(4):
                    i, t = divmod(4 * u + h, 3)
                    at = pl.multiple_of(384 * m + 128 * t, 128)
                    f_ref[32 * i + 8 * ag : 32 * i + 8 * ag + 8, pl.ds(at, 128)] = w[h]
        w = swap4([q_ref[4 * m + q, 64:72, :] for q in range(4)])
        at = pl.multiple_of(384 * m + 256, 128)
        for ag in range(4):
            f_ref[64 + 8 * ag : 64 + 8 * ag + 8, pl.ds(at, 128)] = w[ag]
        return carry

    lax.fori_loop(0, 8, body, 0)
    for k in range(32):
        e_ref[k : k + 1, :] = q_ref[k, 72:73, :]


def unpack(received):
    return pl.pallas_call(
        unpack_kernel,
        out_shape=[jax.ShapeDtypeStruct((96, AUX), f32), jax.ShapeDtypeStruct((32, 128), f32)],
        compiler_params=params(),
        name="unpack_fitted",
    )(received)


def batch_kernel(n_b, has_acc, split_out, *refs):
    idx_ref, pairs_ref, oe_ref, e_ref = refs[:4]
    refs = list(refs[4:])
    a_refs = refs[:5]
    b_refs = refs[5 : 5 + n_b]
    pos = 5 + n_b
    acc_ref = None
    if has_acc:
        acc_ref = refs[pos]
        pos += 1
    outs = refs[pos:-6]
    ahi, alo, bst, c_ref, whi, wlo = refs[-6:]
    row = 0
    for ref in a_refs:
        n = ref.shape[0]
        hi, lo = split(ref[...])
        ahi[row : row + n, :] = hi
        alo[row : row + n, :] = lo
        row += n
    done = 0
    for ref in b_refs:
        for r in range(ref.shape[0] // 32):
            shard, j = divmod(done, 3)
            done += 1
            hi, lo = split(ref[32 * r : 32 * r + 32, :])
            to = 128 * j + 32 * shard
            bst[to : to + 32, :] = hi
            bst[384 + to : 384 + to + 32, :] = lo
    nt = (((1,), (1,)), ((), ()))

    def coulomb_step(k, carry):
        at = pl.ds(pl.multiple_of(k * 512, 512), 512)
        both = lax.dot_general(ahi[:, at], bst[:, at], nt, preferred_element_type=f32)
        part = both[:, :384] + both[:, 384:]
        part += lax.dot_general(alo[:, at], bst[:384, at], nt, preferred_element_type=f32)
        c_ref[...] += part
        return carry

    c_ref[...] = jnp.zeros_like(c_ref)
    lax.fori_loop(0, AUX // 512, coulomb_step, 0)

    lane = lax.broadcasted_iota(jnp.int32, (1, 128), 1)
    square = lax.broadcasted_iota(jnp.int32, (32, 128), 0) == lax.broadcasted_iota(jnp.int32, (32, 128), 1)
    eb = jnp.zeros((1, 128), f32)
    for shard in range(4):
        piece = e_ref[pl.ds(idx_ref[4 + shard], 1), :]
        eb = jnp.where(lane // 32 == shard, piece, eb)
    for d in range(4):
        ea = jnp.sum(jnp.where(square, e_ref[pl.ds(idx_ref[d], 1), :], 0.0), axis=1, keepdims=True)
        for i in range(3):
            for j in range(3):
                rows = slice(96 * d + 32 * i, 96 * d + 32 * i + 32)
                direct = c_ref[rows, 128 * j : 128 * j + 128]
                other = c_ref[96 * d + 32 * j : 96 * d + 32 * j + 32, 128 * i : 128 * i + 128]
                chosen = jnp.int32(0)
                for n in range(6):
                    chosen += ((pairs_ref[n, 0] == i) & (pairs_ref[n, 1] == j)).astype(jnp.int32)
                denominator = (oe_ref[i] + oe_ref[j]) - ea - eb
                w = chosen.astype(f32) * ((2.0 * direct - other) / denominator)
                hi, lo = split(w)
                whi[rows, 128 * j : 128 * j + 128] = hi
                whi[rows, 384 + 128 * j : 384 + 128 * j + 128] = hi
                wlo[rows, 128 * j : 128 * j + 128] = lo

    def gamma_step(k, carry):
        at = pl.ds(pl.multiple_of(k * 512, 512), 512)
        g = jnp.dot(whi[...], bst[:, at], preferred_element_type=f32)
        g += jnp.dot(wlo[...], bst[:384, at], preferred_element_type=f32)
        if has_acc:
            g += acc_ref[:, at]
        row = 0
        for out in outs:
            n = out.shape[0]
            out[:, at] = g[row : row + n]
            row += n
        return carry

    lax.fori_loop(0, AUX // 512, gamma_step, 0)


def batch(idx, pairs, occ_energy, energies, a_list, b_list, acc, out_rows):
    smem = pl.BlockSpec(memory_space=pltpu.SMEM)
    vmem = pl.BlockSpec(memory_space=pltpu.VMEM)
    args = [idx, pairs, occ_energy, energies] + list(a_list) + list(b_list)
    specs = [smem, smem, smem, vmem] + [vmem] * (len(a_list) + len(b_list))
    if acc is not None:
        args.append(acc)
        specs.append(vmem)

    def body(*refs):
        batch_kernel(len(b_list), acc is not None, False, *refs)

    return pl.pallas_call(
        body,
        in_specs=specs,
        out_specs=[vmem] * len(out_rows),
        out_shape=[jax.ShapeDtypeStruct((n, AUX), f32) for n in out_rows],
        scratch_shapes=[
            pltpu.VMEM((384, AUX), bf16),
            pltpu.VMEM((384, AUX), bf16),
            pltpu.VMEM((768, AUX), bf16),
            pltpu.VMEM((384, 384), f32),
            pltpu.VMEM((384, 768), bf16),
            pltpu.VMEM((384, 384), bf16),
        ],
        compiler_params=params(),
        name="gamma_batch_last" if acc is not None else "gamma_batch_first",
    )(*args)


def take_from(x, axis, step):
    n = lax.axis_size(axis)
    return lax.ppermute(x, axis, [(i, (i - step) % n) for i in range(n)])


def local(half_rows, screen, slot_shell, vir_coeff, occ_energy, vir_energy, pair_list):
    packed = pack(half_rows, screen)
    moved = lax.all_to_all(packed.reshape(128, 72, 128), ALL, 0, 0, tiled=True)
    chi, clo = coeff(vir_coeff)
    slots = lax.broadcasted_iota(jnp.int32, (NSH, 512), 1)
    shells = lax.broadcasted_iota(jnp.int32, (NSH, 512), 0)
    inv = jnp.sum(jnp.where(slot_shell[None, :] == shells, slots, 0), axis=1)
    energy_row = jnp.tile(vir_energy, 4).reshape(1, 128)
    sent = transform(inv, moved, energy_row, chi, clo)
    received = lax.all_to_all(sent, GROUP, 0, 0, tiled=True)
    own, energies = unpack(received)

    y1 = take_from(own, "y", 1)
    y3 = take_from(own, "y", -1)
    z1 = take_from(own, "z", 1)
    z3 = take_from(own, "z", -1)
    x0 = take_from(own, "xh", 1)
    y2a = take_from(y1[:48], "y", 1)
    y2b = take_from(y3[48:], "y", -1)
    z2 = take_from(z3, "z", -1)
    x1 = take_from(x0, "z", 1)
    x3 = take_from(z3, "xh", 1)
    x2a = take_from(z2[:32], "xh", 1)
    x2b = take_from(x1[32:64], "z", 1)
    x2c = take_from(x3[64:], "z", -1)

    y = lax.axis_index("y")
    z = lax.axis_index("z")
    xh = lax.axis_index("xh")

    def place(dy, dz, dx):
        return ((y + dy) % 4) * 8 + ((z + dz) % 4) * 2 + (xh + dx) % 2

    rows_at = [place(0, 0, 0), place(1, 0, 0), place(3, 0, 0), place(2, 0, 0)]
    first_at = [place(0, 0, 0), place(0, 1, 0), place(0, 3, 0), place(0, 0, 1)]
    last_at = [place(0, 2, 0), place(0, 1, 1), place(0, 3, 1), place(0, 2, 1)]
    a_list = [own, y1, y3, y2a, y2b]
    (acc,) = batch(
        jnp.stack(rows_at + first_at), pair_list, occ_energy, energies, a_list, [own, z1, z3, x0], None, [384]
    )
    g0, g1, g3, g2a, g2b = batch(
        jnp.stack(rows_at + last_at), pair_list, occ_energy, energies, a_list, [z2, x1, x3, x2a, x2b, x2c], acc,
        [96, 96, 96, 48, 48],
    )
    up = take_from(g2a, "y", -1)
    down = take_from(g2b, "y", 1)
    g1 = jnp.concatenate([g1[:48] + up, g1[48:]], axis=0)
    g3 = jnp.concatenate([g3[:48], g3[48:] + down], axis=0)
    from_below = take_from(g1, "y", -1)
    from_above = take_from(g3, "y", 1)
    return (g0 + from_below + from_above).reshape(3, 32, AUX)


def solution(mesh):
    wide = Mesh(mesh.devices.reshape(2, 2, 4, 4, 2), ALL)
    occ = ("xl", "co")
    in_specs = (P(None, ALL, None), P(None, ALL), P(), P(), P(occ), P(GROUP), P(occ, None))
    out_specs = P(occ, GROUP, None)
    return jax.shard_map(local, mesh=wide, in_specs=in_specs, out_specs=out_specs, check_vma=False)
```

```python
import jax
import jax.numpy as jnp
from jax import lax
from jax.experimental import pallas as pl
from jax.experimental.pallas import tpu as pltpu
from jax.sharding import Mesh, PartitionSpec as P

NVIR = 1024
SHW = 8
NSH = 144
ROWS = NSH * SHW
AUX = 3072
ALL = ("xl", "co", "y", "z", "xh")
GROUP = ("y", "z", "xh")
VLIM = 60 * 1024 * 1024
f32 = jnp.float32
bf16 = jnp.bfloat16


def params():
    return pltpu.CompilerParams(vmem_limit_bytes=VLIM)


def swap4(v):
    lane = lax.broadcasted_iota(jnp.int32, v[0].shape, 1)
    low = lane < 64
    even = (lane // 32) % 2 == 0
    a0 = jnp.where(low, v[0], pltpu.roll(v[2], 64, 1))
    a2 = jnp.where(low, pltpu.roll(v[0], 64, 1), v[2])
    a1 = jnp.where(low, v[1], pltpu.roll(v[3], 64, 1))
    a3 = jnp.where(low, pltpu.roll(v[1], 64, 1), v[3])
    w0 = jnp.where(even, a0, pltpu.roll(a1, 32, 1))
    w1 = jnp.where(even, pltpu.roll(a0, 96, 1), a1)
    w2 = jnp.where(even, a2, pltpu.roll(a3, 32, 1))
    w3 = jnp.where(even, pltpu.roll(a2, 96, 1), a3)
    return w0, w1, w2, w3


def mix4(v):
    lane = lax.broadcasted_iota(jnp.int32, v[0].shape, 1)
    low = lane < 64
    first = lane < 32
    third = lane < 96
    out = []
    for q in range(4):
        p = [v[(n - q) % 4] for n in range(4)]
        out.append(jnp.where(low, jnp.where(first, p[0], p[1]), jnp.where(third, p[2], p[3])))
    return out


def split(x):
    hi = x.astype(bf16)
    lo = (x - hi.astype(f32)).astype(bf16)
    return hi, lo


def pack_kernel(scr_ref, x_ref, o_ref):
    for g in range(4):
        for s in range(4):
            for u in range(2):
                v = []
                for h in range(4):
                    i, t = divmod(4 * u + h, 3)
                    keep = scr_ref[s, 3 * g + i].astype(f32)
                    v.append(x_ref[3 * g + i, 8 * s : 8 * s + 8, 128 * t : 128 * t + 128] * keep)
                w = mix4(v)
                for q in range(4):
                    o_ref[g, q, 8 * (2 * s + u) : 8 * (2 * s + u) + 8, :] = w[q]
        v = []
        for s in range(4):
            keep = scr_ref[s, 3 * g + 2].astype(f32)
            v.append(x_ref[3 * g + 2, 8 * s : 8 * s + 8, 256:384] * keep)
        w = swap4(v)
        for q in range(4):
            o_ref[g, q, 64:72, :] = w[q]


def pack(half_rows, screen):
    return pl.pallas_call(
        pack_kernel,
        grid=(8,),
        in_specs=[
            pl.BlockSpec(memory_space=pltpu.SMEM),
            pl.BlockSpec((12, 32, 384), lambda m: (0, 0, m)),
        ],
        out_specs=pl.BlockSpec((4, 4, 72, 128), lambda m: (0, m, 0, 0)),
        out_shape=jax.ShapeDtypeStruct((4, 32, 72, 128), f32),
        compiler_params=params(),
        name="pack_rows",
    )(screen.T, half_rows)


def coeff_kernel(c_ref, hi_ref, lo_ref):
    hi, lo = split(c_ref[...].T)
    hi_ref[...] = hi
    lo_ref[...] = lo


def coeff(vir_coeff):
    return pl.pallas_call(
        coeff_kernel,
        grid=(9,),
        in_specs=[pl.BlockSpec((128, NVIR), lambda k: (k, 0))],
        out_specs=[pl.BlockSpec((NVIR, 128), lambda k: (0, k))] * 2,
        out_shape=[jax.ShapeDtypeStruct((NVIR, ROWS), bf16)] * 2,
        compiler_params=params(),
        name="split_coeff",
    )(vir_coeff)


def transform_kernel(inv_ref, r_ref, ve_ref, chi_ref, clo_ref, o_ref, xs):
    @pl.when(pl.program_id(0) == 0)
    def _():
        def body(h, carry):
            tiles = []
            for e in range(2):
                where = inv_ref[2 * h + e]
                owner = where // 4
                slot = where % 4
                at = pl.multiple_of(slot * 16, 16)
                t01 = r_ref[owner, pl.ds(at, 16), :]
                t2 = pltpu.roll(r_ref[owner, 64:72, :], (128 - 32 * slot) % 128, 1)
                tiles.append((t01[:8], t01[8:], t2))
            row = pl.multiple_of(h * 16, 16)
            for n in range(3):
                hi, lo = split(jnp.concatenate([tiles[0][n], tiles[1][n]], axis=0))
                xs[pl.ds(row, 16), 128 * n : 128 * n + 128] = hi
                xs[pl.ds(row, 16), 384 + 128 * n : 512 + 128 * n] = lo
            return carry

        lax.fori_loop(0, NSH // 2, body, 0, unroll=4)

    both = jnp.dot(chi_ref[...], xs[...], preferred_element_type=f32)
    y = both[:, :384] + both[:, 384:]
    y += jnp.dot(clo_ref[...], xs[:, :384], preferred_element_type=f32)
    lane = lax.broadcasted_iota(jnp.int32, (8, 128), 1) // 32
    for k in range(16):
        last = jnp.zeros((8, 128), f32)
        for ag in range(4):
            rows = slice(32 * k + 8 * ag, 32 * k + 8 * ag + 8)
            for u in range(2):
                o_ref[k, 8 * (2 * ag + u) : 8 * (2 * ag + u) + 8, :] = y[rows, 128 * u : 128 * u + 128]
            piece = y[rows, 256:384]
            if ag:
                piece = pltpu.roll(piece, 32 * ag, 1)
            last = jnp.where(lane == ag, piece, last)
        o_ref[k, 64:72, :] = last
        o_ref[k, 72:80, :] = jnp.broadcast_to(ve_ref[...], (8, 128))


def transform(inv, rows, energy_row, chi, clo):
    return pl.pallas_call(
        transform_kernel,
        grid=(2,),
        in_specs=[
            pl.BlockSpec(memory_space=pltpu.SMEM),
            pl.BlockSpec((128, 72, 128), lambda m: (0, 0, 0)),
            pl.BlockSpec((1, 128), lambda m: (0, 0)),
            pl.BlockSpec((512, ROWS), lambda m: (m, 0)),
            pl.BlockSpec((512, ROWS), lambda m: (m, 0)),
        ],
        out_specs=pl.BlockSpec((16, 80, 128), lambda m: (m, 0, 0)),
        out_shape=jax.ShapeDtypeStruct((32, 80, 128), f32),
        scratch_shapes=[pltpu.VMEM((ROWS, 768), bf16)],
        compiler_params=params(),
        name="transform_rows",
    )(inv, rows, energy_row, chi, clo)


def unpack_kernel(at_ref, q_ref, f_ref, e_ref):
    for n in range(12):
        e_ref[n : n + 1, :] = q_ref[at_ref[n], 72:73, :]

    def body(m, carry):
        for ag in range(4):
            for u in range(2):
                w = mix4([q_ref[4 * m + q, 8 * (2 * ag + u) : 8 * (2 * ag + u) + 8, :] for q in range(4)])
                for h in range(4):
                    i, t = divmod(4 * u + h, 3)
                    at = pl.multiple_of(384 * m + 128 * t, 128)
                    f_ref[32 * i + 8 * ag : 32 * i + 8 * ag + 8, pl.ds(at, 128)] = w[h]
        w = swap4([q_ref[4 * m + q, 64:72, :] for q in range(4)])
        at = pl.multiple_of(384 * m + 256, 128)
        for ag in range(4):
            f_ref[64 + 8 * ag : 64 + 8 * ag + 8, pl.ds(at, 128)] = w[ag]
        return carry

    lax.fori_loop(0, 8, body, 0)


def unpack(places, received):
    return pl.pallas_call(
        unpack_kernel,
        in_specs=[pl.BlockSpec(memory_space=pltpu.SMEM), pl.BlockSpec(memory_space=pltpu.VMEM)],
        out_shape=[jax.ShapeDtypeStruct((96, AUX), f32), jax.ShapeDtypeStruct((12, 128), f32)],
        compiler_params=params(),
        name="unpack_fitted",
    )(places, received)


def block_kernel(n_a, n_b, n_acc, n_out, shards, row_at, col_at, *refs):
    pairs_ref, oe_ref, e_ref = refs[:3]
    a_refs = refs[3 : 3 + n_a]
    b_refs = refs[3 + n_a : 3 + n_a + n_b]
    acc_refs = refs[3 + n_a + n_b : 3 + n_a + n_b + n_acc]
    outs = refs[3 + n_a + n_b + n_acc : 3 + n_a + n_b + n_acc + n_out]
    a_in, b_in, g_buf, ahi, alo, bst, c_ref, whi, wlo, a_sem, b_sem, acc_sem, out_sem = refs[-13:]
    wide = shards > 1
    width = 384 if wide else 128
    rows_total = ahi.shape[0]

    def into(group, buf, sem):
        copies = []
        row = 0
        for n, ref in enumerate(group):
            h = ref.shape[0]
            copies.append((pltpu.make_async_copy(ref, buf.at[row : row + h], sem.at[n]), row, h))
            row += h
        for copy, _, _ in copies:
            copy.start()
        return copies

    a_copies = into(a_refs, a_in, a_sem)
    b_copies = into(b_refs, b_in, b_sem)
    acc_copies = into(acc_refs, g_buf, acc_sem)
    for copy, row, h in a_copies:
        copy.wait()
        for r in range(row, row + h, 16):
            hi, lo = split(a_in[r : r + 16, :])
            ahi[r : r + 16, :] = hi
            alo[r : r + 16, :] = lo
    for copy, row, h in b_copies:
        copy.wait()
        for r in range(row, row + h, 32):
            shard, j = divmod(r // 32, 3)
            hi, lo = split(b_in[r : r + 32, :])
            to = 128 * j + 32 * shard if wide else 32 * j
            bst[to : to + 32, :] = hi
            bst[width + to : width + to + 32, :] = lo
    blank = [128 * j + 32 * shard for j in range(3) for shard in range(shards, 4)] if wide else [96]
    for to in blank:
        bst[to : to + 32, :] = jnp.zeros((32, AUX), bf16)
        bst[width + to : width + to + 32, :] = jnp.zeros((32, AUX), bf16)
    nt = (((1,), (1,)), ((), ()))

    def coulomb_step(k, carry):
        at = pl.ds(pl.multiple_of(k * 512, 512), 512)
        both = lax.dot_general(ahi[:, at], bst[:, at], nt, preferred_element_type=f32)
        part = both[:, :width] + both[:, width:]
        part += lax.dot_general(alo[:, at], bst[:width, at], nt, preferred_element_type=f32)
        c_ref[...] += part
        return carry

    c_ref[...] = jnp.zeros_like(c_ref)
    lax.fori_loop(0, AUX // 512, coulomb_step, 0)

    group = lax.broadcasted_iota(jnp.int32, (1, 128), 1) // 32
    square = lax.broadcasted_iota(jnp.int32, (32, 128), 0) == lax.broadcasted_iota(jnp.int32, (32, 128), 1)
    chosen = []
    for i in range(3):
        for j in range(3):
            count = jnp.int32(0)
            for n in range(6):
                count += ((pairs_ref[0, n] == i) & (pairs_ref[1, n] == j)).astype(jnp.int32)
            chosen.append(count.astype(f32))
    col = jnp.zeros((1, 128), f32)
    if wide:
        for shard in range(shards):
            col = jnp.where(group == shard, e_ref[col_at + shard : col_at + shard + 1, :], col)
    else:
        piece = e_ref[col_at : col_at + 1, :]
        for j in range(3):
            col = jnp.where(group == j, piece - oe_ref[j], col)
    for d in range(rows_total // 96):
        ea = jnp.sum(jnp.where(square, e_ref[row_at[d] : row_at[d] + 1, :], 0.0), axis=1, keepdims=True)
        for i in range(3):
            rows = slice(96 * d + 32 * i, 96 * d + 32 * i + 32)
            if wide:
                for j in range(3):
                    direct = c_ref[rows, 128 * j : 128 * j + 128]
                    other = c_ref[96 * d + 32 * j : 96 * d + 32 * j + 32, 128 * i : 128 * i + 128]
                    denominator = (oe_ref[i] + oe_ref[j]) - ea - col
                    hi, lo = split(chosen[3 * i + j] * ((2.0 * direct - other) / denominator))
                    whi[rows, 128 * j : 128 * j + 128] = hi
                    whi[rows, 384 + 128 * j : 512 + 128 * j] = hi
                    wlo[rows, 128 * j : 128 * j + 128] = lo
            else:
                direct = c_ref[rows, :]
                other = jnp.zeros((32, 128), f32)
                keep = jnp.zeros((1, 128), f32)
                for j in range(3):
                    moved = c_ref[96 * d + 32 * j : 96 * d + 32 * j + 32, :]
                    if j != i:
                        moved = pltpu.roll(moved, (32 * (j - i)) % 128, 1)
                    other = jnp.where(group == j, moved, other)
                    keep = jnp.where(group == j, chosen[3 * i + j], keep)
                denominator = oe_ref[i] - ea - col
                hi, lo = split(keep * ((2.0 * direct - other) / denominator))
                whi[rows, :128] = hi
                whi[rows, 128:] = hi
                wlo[rows, :] = lo

    for copy, _, _ in acc_copies:
        copy.wait()

    def out_copies(k):
        at = pl.ds(pl.multiple_of(k * 512, 512), 512)
        row = 0
        for n, out in enumerate(outs):
            h = out.shape[0]
            yield pltpu.make_async_copy(g_buf.at[row : row + h, at], out.at[:, at], out_sem.at[k, n])
            row += h

    def gamma_step(k, carry):
        at = pl.ds(pl.multiple_of(k * 512, 512), 512)
        g = jnp.dot(whi[...], bst[:, at], preferred_element_type=f32)
        g += jnp.dot(wlo[...], bst[:width, at], preferred_element_type=f32)
        if n_acc:
            g += g_buf[:, at]
        g_buf[:, at] = g
        for copy in out_copies(k):
            copy.start()
        return carry

    lax.fori_loop(0, AUX // 512, gamma_step, 0)
    for k in range(AUX // 512):
        for copy in out_copies(k):
            copy.wait()


def block(name, tables, a_list, row_at, b_list, col_at, acc_list, out_rows):
    a_list = list(a_list)
    b_list = list(b_list)
    smem = pl.BlockSpec(memory_space=pltpu.SMEM)
    vmem = pl.BlockSpec(memory_space=pltpu.VMEM)
    hbm = pl.BlockSpec(memory_space=pl.ANY)
    rows = sum(a.shape[0] for a in a_list)
    shards = sum(b.shape[0] for b in b_list) // 96
    width = 384 if shards > 1 else 128
    args = list(tables) + a_list + b_list + list(acc_list)
    counts = (len(a_list), len(b_list), len(acc_list), len(out_rows), shards, row_at, col_at)

    def body(*refs):
        block_kernel(*counts, *refs)

    dma = pltpu.SemaphoreType.DMA
    return pl.pallas_call(
        body,
        in_specs=[smem, smem, vmem] + [hbm] * (len(args) - 3),
        out_specs=[hbm] * len(out_rows),
        out_shape=[jax.ShapeDtypeStruct((n, AUX), f32) for n in out_rows],
        scratch_shapes=[
            pltpu.VMEM((rows, AUX), f32),
            pltpu.VMEM((96 * shards, AUX), f32),
            pltpu.VMEM((rows, AUX), f32),
            pltpu.VMEM((rows, AUX), bf16),
            pltpu.VMEM((rows, AUX), bf16),
            pltpu.VMEM((2 * width, AUX), bf16),
            pltpu.VMEM((rows, width), f32),
            pltpu.VMEM((rows, 2 * width), bf16),
            pltpu.VMEM((rows, width), bf16),
            dma((len(a_list),)),
            dma((len(b_list),)),
            dma((max(len(acc_list), 1),)),
            dma((AUX // 512, len(out_rows))),
        ],
        compiler_params=pltpu.CompilerParams(vmem_limit_bytes=36 * 1024 * 1024),
        cost_estimate=pl.CostEstimate(
            flops=2 * rows * width * AUX * 6, transcendentals=0, bytes_accessed=4 * AUX * (2 * rows + 96 * shards)
        ),
        name=name,
    )(*args)


def take_from(x, axis, step):
    n = lax.axis_size(axis)
    return lax.ppermute(x, axis, [(i, (i - step) % n) for i in range(n)])


def local(half_rows, screen, slot_shell, vir_coeff, occ_energy, vir_energy, pair_list):
    packed = pack(half_rows, screen)
    moved = lax.all_to_all(packed.reshape(128, 72, 128), ALL, 0, 0, tiled=True)
    chi, clo = coeff(vir_coeff)
    slots = lax.broadcasted_iota(jnp.int32, (NSH, 512), 1)
    shells = lax.broadcasted_iota(jnp.int32, (NSH, 512), 0)
    inv = jnp.sum(jnp.where(slot_shell[None, :] == shells, slots, 0), axis=1)
    y = lax.axis_index("y")
    z = lax.axis_index("z")
    xh = lax.axis_index("xh")

    def place(dy, dz, dx):
        return (y + dy) % 4 * 8 + (z + dz) % 4 * 2 + (xh + dx) % 2

    places = jnp.stack(
        [place(dy, 0, 0) for dy in (0, 1, 3, 2)]
        + [place(0, 0, 0), place(0, 1, 0), place(0, 3, 0), place(0, 0, 1)]
        + [place(0, 2, 0), place(0, 1, 1), place(0, 3, 1), place(0, 2, 1)]
    ).astype(jnp.int32)
    energy_row = jnp.tile(vir_energy, 4).reshape(1, 128)
    moved, inv, places, energy_row = lax.optimization_barrier((moved, inv, places, energy_row))
    sent = transform(inv, moved, energy_row, chi, clo)
    received = lax.all_to_all(sent, GROUP, 0, 0, tiled=True)
    own, energies = unpack(places, received)
    tables = (pair_list.T, occ_energy, energies)
    here, above, below, across = 0, 1, 2, 3

    y1 = take_from(own, "y", 1)
    y3 = take_from(own, "y", -1)
    z1 = take_from(own, "z", 1)
    z3 = take_from(own, "z", -1)
    x0 = take_from(own, "xh", 1)
    y1, y3, z1, z3, x0 = lax.optimization_barrier((y1, y3, z1, z3, x0))
    y2a = take_from(y1[:48], "y", 1)
    y2b = take_from(y3[48:], "y", -1)
    z2 = take_from(z3, "z", -1)
    x1 = take_from(x0, "z", 1)
    x3 = take_from(z3, "xh", 1)
    cols = [own, z1, z3, x0]
    rows, rows_at = [own, y1, y3, y2a, y2b], (here, above, below, across)
    own_acc, near_acc, far_acc = block("gamma_first", tables, rows, rows_at, cols, 4, [], [96, 192, 96])
    z2, x1, x3, own_acc, near_acc, far_acc = lax.optimization_barrier((z2, x1, x3, own_acc, near_acc, far_acc))
    x2a = take_from(z2[:32], "xh", 1)
    x2b = take_from(x1[32:64], "z", 1)
    x2c = take_from(x3[64:], "z", -1)
    own_acc, near_acc, far_acc = block(
        "gamma_next", tables, rows, rows_at, [z2, x1, x3], 8, [own_acc, near_acc, far_acc], [96, 192, 96]
    )
    tail = [x2a, x2b, x2c]
    g2a, g2b = block("gamma_far", tables, [y2a, y2b], (across,), tail, 11, [far_acc], [48, 48])
    up = take_from(g2a, "y", -1)
    down = take_from(g2b, "y", 1)
    g1a, g1b, g3a, g3b = block(
        "gamma_near", tables, [y1, y3], (above, below), tail, 11, [near_acc], [48, 48, 48, 48]
    )
    below_b = take_from(g1b, "y", -1)
    above_a = take_from(g3a, "y", 1)
    (g0,) = block("gamma_own", tables, [own], (here,), tail, 11, [own_acc], [96])
    below_a = take_from(g1a + up, "y", -1)
    above_b = take_from(g3b + down, "y", 1)
    from_below = jnp.concatenate([below_a, below_b], axis=0)
    from_above = jnp.concatenate([above_a, above_b], axis=0)
    return (g0 + from_below + from_above).reshape(3, 32, AUX)


def solution(mesh):
    wide = Mesh(mesh.devices.reshape(2, 2, 4, 4, 2), ALL)
    occ = ("xl", "co")
    in_specs = (P(None, ALL, None), P(None, ALL), P(), P(), P(occ), P(GROUP), P(occ, None))
    out_specs = P(occ, GROUP, None)
    return jax.shard_map(local, mesh=wide, in_specs=in_specs, out_specs=out_specs, check_vma=False)
```

```python
import jax
import jax.numpy as jnp
from jax import lax
from jax.experimental import pallas as pl
from jax.experimental.pallas import tpu as pltpu
from jax.sharding import Mesh, PartitionSpec as P

NVIR = 1024
SHW = 8
NSH = 144
ROWS = NSH * SHW
AUX = 3072
ALL = ("xl", "co", "y", "z", "xh")
GROUP = ("y", "z", "xh")
DEPTH = 1536
VLIM = 60 * 1024 * 1024
f32 = jnp.float32
bf16 = jnp.bfloat16


def params():
    return pltpu.CompilerParams(vmem_limit_bytes=VLIM)


def swap4(v):
    lane = lax.broadcasted_iota(jnp.int32, v[0].shape, 1)
    low = lane < 64
    even = (lane // 32) % 2 == 0
    a0 = jnp.where(low, v[0], pltpu.roll(v[2], 64, 1))
    a2 = jnp.where(low, pltpu.roll(v[0], 64, 1), v[2])
    a1 = jnp.where(low, v[1], pltpu.roll(v[3], 64, 1))
    a3 = jnp.where(low, pltpu.roll(v[1], 64, 1), v[3])
    w0 = jnp.where(even, a0, pltpu.roll(a1, 32, 1))
    w1 = jnp.where(even, pltpu.roll(a0, 96, 1), a1)
    w2 = jnp.where(even, a2, pltpu.roll(a3, 32, 1))
    w3 = jnp.where(even, pltpu.roll(a2, 96, 1), a3)
    return w0, w1, w2, w3


def mix4(v):
    lane = lax.broadcasted_iota(jnp.int32, v[0].shape, 1)
    low = lane < 64
    first = lane < 32
    third = lane < 96
    out = []
    for q in range(4):
        p = [v[(n - q) % 4] for n in range(4)]
        out.append(jnp.where(low, jnp.where(first, p[0], p[1]), jnp.where(third, p[2], p[3])))
    return out


def split(x):
    hi = x.astype(bf16)
    lo = (x - hi.astype(f32)).astype(bf16)
    return hi, lo


def map_kernel(me_ref, row_ref, col_ref, o_ref):
    def parts(g):
        owner = g // 4
        chip = owner // 64 * 32 + owner % 32
        return chip, owner // 32 % 2 * 4 + g % 4

    here, at = parts(lax.broadcasted_iota(jnp.int32, (512, 1), 0))
    there, other = parts(lax.broadcasted_iota(jnp.int32, (1, 512), 1))
    taken = (row_ref[...] >= 0).astype(jnp.int32)
    mates = jnp.where(here == there, taken, 0)
    count = jnp.sum(mates, axis=1, keepdims=True)
    rank = jnp.sum(jnp.where(other < at, mates, 0), axis=1, keepdims=True)
    shell = col_ref[...]
    lane = lax.broadcasted_iota(jnp.int32, (1, 256), 1)
    place = jnp.sum(jnp.where(shell == lane, here * 8 + rank, 0), axis=0, keepdims=True)
    mine = (here == me_ref[0]) & (shell >= 0) & (rank == lane)
    order = jnp.sum(jnp.where(mine, at, 0), axis=0, keepdims=True)
    most = jnp.max(count, axis=0, keepdims=True)
    o_ref[...] = jnp.zeros_like(o_ref)
    o_ref[0:1, :] = place
    o_ref[1:2, :] = order
    o_ref[2:3, :] = jnp.broadcast_to(most, (1, 256))


def slot_map(me, slot_shell):
    vmem = pl.BlockSpec(memory_space=pltpu.VMEM)
    return pl.pallas_call(
        map_kernel,
        in_specs=[pl.BlockSpec(memory_space=pltpu.SMEM), vmem, vmem],
        out_shape=jax.ShapeDtypeStruct((8, 256), jnp.int32),
        compiler_params=pltpu.CompilerParams(vmem_limit_bytes=16 * 1024 * 1024),
        name="slot_map",
    )(me, slot_shell.reshape(1, 512), slot_shell.reshape(512, 1))


def gift_kernel(me_ref, scr_ref, x_ref, o_ref):
    g = pl.program_id(0)
    co = me_ref[1]
    for i in range(3):
        for s in range(4):
            keep = scr_ref[s, (2 * g + 1 - co) * 3 + i].astype(f32)
            rows = slice(32 * i + 8 * s, 32 * i + 8 * s + 8)
            o_ref[0, rows, :] = x_ref[0, 0, rows, :] * keep


def gift(me, screen_t, rows):
    return pl.pallas_call(
        gift_kernel,
        grid_spec=pltpu.PrefetchScalarGridSpec(
            num_scalar_prefetch=2,
            grid=(2, 2),
            in_specs=[pl.BlockSpec((1, 1, 96, 1536), lambda g, n, me, scr: (g, 1 - me[1], 0, n))],
            out_specs=pl.BlockSpec((1, 96, 1536), lambda g, n, me, scr: (g, 0, n)),
        ),
        out_shape=jax.ShapeDtypeStruct((2, 96, AUX), f32),
        compiler_params=params(),
        name="gift_rows",
    )(me, screen_t, rows)


def message_rows(cap):
    return 16 * cap + 8 * ((cap + 3) // 4)


def pack_kernel(cap, me_ref, scr_ref, map_ref, x_ref, y_ref, o_ref):
    co = me_ref[1]
    for g in range(2):

        def part(p, i, t):
            place = map_ref[1, p]
            s = place % 4
            at = pl.ds(pl.multiple_of(32 * i + 8 * s, 8), 8)
            cols = slice(128 * t, 128 * t + 128)
            keep = scr_ref[s, (2 * g + co) * 3 + i].astype(f32)
            return jnp.where(place // 4 == co, x_ref[g, 0, at, cols] * keep, y_ref[g, at, cols])

        for p in range(cap):
            for u in range(2):
                w = mix4([part(p, *divmod(4 * u + h, 3)) for h in range(4)])
                for q in range(4):
                    o_ref[g, q, 8 * (2 * p + u) : 8 * (2 * p + u) + 8, :] = w[q]
        for four in range((cap + 3) // 4):
            w = swap4([part(min(4 * four + n, cap - 1), 2, 2) for n in range(4)])
            to = 16 * cap + 8 * four
            for q in range(4):
                o_ref[g, q, to : to + 8, :] = w[q]


def pack(cap, me, screen_t, meta, rows, given):
    size = message_rows(cap)

    def body(*refs):
        pack_kernel(cap, *refs)

    return pl.pallas_call(
        body,
        grid_spec=pltpu.PrefetchScalarGridSpec(
            num_scalar_prefetch=3,
            grid=(8,),
            in_specs=[
                pl.BlockSpec((2, 1, 96, 384), lambda m, me, scr, mp: (0, me[1], 0, m)),
                pl.BlockSpec((2, 96, 384), lambda m, me, scr, mp: (0, 0, m)),
            ],
            out_specs=pl.BlockSpec((2, 4, size, 128), lambda m, me, scr, mp: (0, m, 0, 0)),
        ),
        out_shape=jax.ShapeDtypeStruct((2, 32, size, 128), f32),
        compiler_params=params(),
        name=f"pack_rows_{cap}",
    )(me, screen_t, meta, rows, given)


def coeff_kernel(c_ref, hi_ref, lo_ref):
    hi, lo = split(c_ref[...].T)
    hi_ref[...] = hi
    lo_ref[...] = lo


def coeff(vir_coeff):
    return pl.pallas_call(
        coeff_kernel,
        grid=(9,),
        in_specs=[pl.BlockSpec((128, NVIR), lambda k: (k, 0))],
        out_specs=[pl.BlockSpec((NVIR, 128), lambda k: (0, k))] * 2,
        out_shape=[jax.ShapeDtypeStruct((NVIR, ROWS), bf16)] * 2,
        compiler_params=params(),
        name="split_coeff",
    )(vir_coeff)


def transform_kernel(cap, map_ref, r_ref, ve_ref, chi_ref, clo_ref, o_ref, xs):
    @pl.when(pl.program_id(0) == 0)
    def _():
        def body(h, carry):
            tiles = []
            for e in range(2):
                where = map_ref[0, 2 * h + e]
                chip = where // 8
                rank = where % 8
                t01 = r_ref[chip, pl.ds(pl.multiple_of(rank * 16, 16), 16), :]
                t2 = r_ref[chip, pl.ds(pl.multiple_of(16 * cap + rank // 4 * 8, 8), 8), :]
                t2 = pltpu.roll(t2, (128 - 32 * (rank % 4)) % 128, 1)
                tiles.append((t01[:8], t01[8:], t2))
            row = pl.multiple_of(h * 16, 16)
            for n in range(3):
                hi, lo = split(jnp.concatenate([tiles[0][n], tiles[1][n]], axis=0))
                xs[pl.ds(row, 16), 128 * n : 128 * n + 128] = hi
                xs[pl.ds(row, 16), 384 + 128 * n : 512 + 128 * n] = lo
            return carry

        lax.fori_loop(0, NSH // 2, body, 0, unroll=4)

    both = jnp.dot(chi_ref[...], xs[...], preferred_element_type=f32)
    y = both[:, :384] + both[:, 384:]
    y += jnp.dot(clo_ref[...], xs[:, :384], preferred_element_type=f32)
    lane = lax.broadcasted_iota(jnp.int32, (8, 128), 1) // 32
    for k in range(16):
        last = jnp.zeros((8, 128), f32)
        for ag in range(4):
            rows = slice(32 * k + 8 * ag, 32 * k + 8 * ag + 8)
            for u in range(2):
                o_ref[k, 8 * (2 * ag + u) : 8 * (2 * ag + u) + 8, :] = y[rows, 128 * u : 128 * u + 128]
            piece = y[rows, 256:384]
            if ag:
                piece = pltpu.roll(piece, 32 * ag, 1)
            last = jnp.where(lane == ag, piece, last)
        o_ref[k, 64:72, :] = last
        o_ref[k, 72:80, :] = jnp.broadcast_to(ve_ref[...], (8, 128))


def transform(cap, meta, rows, energy_row, chi, clo):
    def body(*refs):
        transform_kernel(cap, *refs)

    return pl.pallas_call(
        body,
        grid=(2,),
        in_specs=[
            pl.BlockSpec(memory_space=pltpu.SMEM),
            pl.BlockSpec((64, message_rows(cap), 128), lambda m: (0, 0, 0)),
            pl.BlockSpec((1, 128), lambda m: (0, 0)),
            pl.BlockSpec((512, ROWS), lambda m: (m, 0)),
            pl.BlockSpec((512, ROWS), lambda m: (m, 0)),
        ],
        out_specs=pl.BlockSpec((16, 80, 128), lambda m: (m, 0, 0)),
        out_shape=jax.ShapeDtypeStruct((32, 80, 128), f32),
        scratch_shapes=[pltpu.VMEM((ROWS, 768), bf16)],
        compiler_params=params(),
        name=f"transform_rows_{cap}",
    )(meta, rows, energy_row, chi, clo)


def unpack_kernel(at_ref, q_ref, f_ref, e_ref):
    for n in range(12):
        e_ref[n : n + 1, :] = q_ref[at_ref[n], 72:73, :]

    def body(m, carry):
        for ag in range(4):
            for u in range(2):
                w = mix4([q_ref[4 * m + q, 8 * (2 * ag + u) : 8 * (2 * ag + u) + 8, :] for q in range(4)])
                for h in range(4):
                    i, t = divmod(4 * u + h, 3)
                    at = pl.multiple_of(384 * m + 128 * t, 128)
                    f_ref[32 * i + 8 * ag : 32 * i + 8 * ag + 8, pl.ds(at, 128)] = w[h]
        w = swap4([q_ref[4 * m + q, 64:72, :] for q in range(4)])
        at = pl.multiple_of(384 * m + 256, 128)
        for ag in range(4):
            f_ref[64 + 8 * ag : 64 + 8 * ag + 8, pl.ds(at, 128)] = w[ag]
        return carry

    lax.fori_loop(0, 8, body, 0)


def unpack(places, received):
    return pl.pallas_call(
        unpack_kernel,
        in_specs=[pl.BlockSpec(memory_space=pltpu.SMEM), pl.BlockSpec(memory_space=pltpu.VMEM)],
        out_shape=[jax.ShapeDtypeStruct((96, AUX), f32), jax.ShapeDtypeStruct((12, 128), f32)],
        compiler_params=params(),
        name="unpack_fitted",
    )(places, received)


def block_kernel(n_a, n_b, n_acc, n_out, shards, row_at, col_at, *refs):
    pairs_ref, oe_ref, e_ref = refs[:3]
    a_refs = refs[3 : 3 + n_a]
    b_refs = refs[3 + n_a : 3 + n_a + n_b]
    acc_refs = refs[3 + n_a + n_b : 3 + n_a + n_b + n_acc]
    outs = refs[3 + n_a + n_b + n_acc : 3 + n_a + n_b + n_acc + n_out]
    a_in, b_in, g_buf, ahi, alo, bst, c_ref, whi, wlo, a_sem, b_sem, acc_sem, out_sem = refs[-13:]
    wide = shards > 1
    width = 384 if wide else 128
    rows_total = ahi.shape[0]

    def into(group, buf, sem):
        copies = []
        row = 0
        for n, ref in enumerate(group):
            h = ref.shape[0]
            copies.append((pltpu.make_async_copy(ref, buf.at[row : row + h], sem.at[n]), row, h))
            row += h
        for copy, _, _ in copies:
            copy.start()
        return copies

    a_copies = into(a_refs, a_in, a_sem)
    b_copies = into(b_refs, b_in, b_sem)
    acc_copies = into(acc_refs, g_buf, acc_sem)
    for copy, row, h in a_copies:
        copy.wait()
        for r in range(row, row + h, 16):
            hi, lo = split(a_in[r : r + 16, :])
            ahi[r : r + 16, :] = hi
            alo[r : r + 16, :] = lo
    for copy, row, h in b_copies:
        copy.wait()
        for r in range(row, row + h, 32):
            shard, j = divmod(r // 32, 3)
            hi, lo = split(b_in[r : r + 32, :])
            to = 128 * j + 32 * shard if wide else 32 * j
            bst[to : to + 32, :] = hi
            bst[width + to : width + to + 32, :] = lo
    blank = [128 * j + 32 * shard for j in range(3) for shard in range(shards, 4)] if wide else [96]
    for to in blank:
        bst[to : to + 32, :] = jnp.zeros((32, AUX), bf16)
        bst[width + to : width + to + 32, :] = jnp.zeros((32, AUX), bf16)
    nt = (((1,), (1,)), ((), ()))

    def coulomb_step(k, carry):
        at = pl.ds(pl.multiple_of(k * DEPTH, DEPTH), DEPTH)
        both = lax.dot_general(ahi[:, at], bst[:, at], nt, preferred_element_type=f32)
        part = both[:, :width] + both[:, width:]
        part += lax.dot_general(alo[:, at], bst[:width, at], nt, preferred_element_type=f32)
        c_ref[...] += part
        return carry

    c_ref[...] = jnp.zeros_like(c_ref)
    lax.fori_loop(0, AUX // DEPTH, coulomb_step, 0)

    group = lax.broadcasted_iota(jnp.int32, (1, 128), 1) // 32
    square = lax.broadcasted_iota(jnp.int32, (32, 128), 0) == lax.broadcasted_iota(jnp.int32, (32, 128), 1)
    chosen = []
    for i in range(3):
        for j in range(3):
            count = jnp.int32(0)
            for n in range(6):
                count += ((pairs_ref[0, n] == i) & (pairs_ref[1, n] == j)).astype(jnp.int32)
            chosen.append(count.astype(f32))
    col = jnp.zeros((1, 128), f32)
    if wide:
        for shard in range(shards):
            col = jnp.where(group == shard, e_ref[col_at + shard : col_at + shard + 1, :], col)
    else:
        piece = e_ref[col_at : col_at + 1, :]
        for j in range(3):
            col = jnp.where(group == j, piece - oe_ref[j], col)
    for d in range(rows_total // 96):
        ea = jnp.sum(jnp.where(square, e_ref[row_at[d] : row_at[d] + 1, :], 0.0), axis=1, keepdims=True)
        for i in range(3):
            rows = slice(96 * d + 32 * i, 96 * d + 32 * i + 32)
            if wide:
                for j in range(3):
                    direct = c_ref[rows, 128 * j : 128 * j + 128]
                    other = c_ref[96 * d + 32 * j : 96 * d + 32 * j + 32, 128 * i : 128 * i + 128]
                    denominator = (oe_ref[i] + oe_ref[j]) - ea - col
                    hi, lo = split(chosen[3 * i + j] * ((2.0 * direct - other) / denominator))
                    whi[rows, 128 * j : 128 * j + 128] = hi
                    whi[rows, 384 + 128 * j : 512 + 128 * j] = hi
                    wlo[rows, 128 * j : 128 * j + 128] = lo
            else:
                direct = c_ref[rows, :]
                other = jnp.zeros((32, 128), f32)
                keep = jnp.zeros((1, 128), f32)
                for j in range(3):
                    moved = c_ref[96 * d + 32 * j : 96 * d + 32 * j + 32, :]
                    if j != i:
                        moved = pltpu.roll(moved, (32 * (j - i)) % 128, 1)
                    other = jnp.where(group == j, moved, other)
                    keep = jnp.where(group == j, chosen[3 * i + j], keep)
                denominator = oe_ref[i] - ea - col
                hi, lo = split(keep * ((2.0 * direct - other) / denominator))
                whi[rows, :128] = hi
                whi[rows, 128:] = hi
                wlo[rows, :] = lo

    for copy, _, _ in acc_copies:
        copy.wait()

    def out_copies(k):
        at = pl.ds(pl.multiple_of(k * 512, 512), 512)
        row = 0
        for n, out in enumerate(outs):
            h = out.shape[0]
            yield pltpu.make_async_copy(g_buf.at[row : row + h, at], out.at[:, at], out_sem.at[k, n])
            row += h

    def gamma_step(k, carry):
        at = pl.ds(pl.multiple_of(k * 512, 512), 512)
        g = jnp.dot(whi[...], bst[:, at], preferred_element_type=f32)
        g += jnp.dot(wlo[...], bst[:width, at], preferred_element_type=f32)
        if n_acc:
            g += g_buf[:, at]
        g_buf[:, at] = g
        for copy in out_copies(k):
            copy.start()
        return carry

    lax.fori_loop(0, AUX // 512, gamma_step, 0)
    for k in range(AUX // 512):
        for copy in out_copies(k):
            copy.wait()


def block(name, tables, a_list, row_at, b_list, col_at, acc_list, out_rows):
    a_list = list(a_list)
    b_list = list(b_list)
    smem = pl.BlockSpec(memory_space=pltpu.SMEM)
    vmem = pl.BlockSpec(memory_space=pltpu.VMEM)
    hbm = pl.BlockSpec(memory_space=pl.ANY)
    rows = sum(a.shape[0] for a in a_list)
    shards = sum(b.shape[0] for b in b_list) // 96
    width = 384 if shards > 1 else 128
    args = list(tables) + a_list + b_list + list(acc_list)
    counts = (len(a_list), len(b_list), len(acc_list), len(out_rows), shards, row_at, col_at)

    def body(*refs):
        block_kernel(*counts, *refs)

    dma = pltpu.SemaphoreType.DMA
    return pl.pallas_call(
        body,
        in_specs=[smem, smem, vmem] + [hbm] * (len(args) - 3),
        out_specs=[hbm] * len(out_rows),
        out_shape=[jax.ShapeDtypeStruct((n, AUX), f32) for n in out_rows],
        scratch_shapes=[
            pltpu.VMEM((rows, AUX), f32),
            pltpu.VMEM((96 * shards, AUX), f32),
            pltpu.VMEM((rows, AUX), f32),
            pltpu.VMEM((rows, AUX), bf16),
            pltpu.VMEM((rows, AUX), bf16),
            pltpu.VMEM((2 * width, AUX), bf16),
            pltpu.VMEM((rows, width), f32),
            pltpu.VMEM((rows, 2 * width), bf16),
            pltpu.VMEM((rows, width), bf16),
            dma((len(a_list),)),
            dma((len(b_list),)),
            dma((max(len(acc_list), 1),)),
            dma((AUX // 512, len(out_rows))),
        ],
        compiler_params=pltpu.CompilerParams(vmem_limit_bytes=36 * 1024 * 1024),
        cost_estimate=pl.CostEstimate(
            flops=2 * rows * width * AUX * 6, transcendentals=0, bytes_accessed=4 * AUX * (2 * rows + 96 * shards)
        ),
        name=name,
    )(*args)


def take_from(x, axis, step):
    n = lax.axis_size(axis)
    return lax.ppermute(x, axis, [(i, (i - step) % n) for i in range(n)])


def local(half_rows, screen, slot_shell, vir_coeff, occ_energy, vir_energy, pair_list):
    y = lax.axis_index("y")
    z = lax.axis_index("z")
    xh = lax.axis_index("xh")

    def place(dy, dz, dx):
        return (y + dy) % 4 * 8 + (z + dz) % 4 * 2 + (xh + dx) % 2

    places = jnp.stack(
        [place(dy, 0, 0) for dy in (0, 1, 3, 2)]
        + [place(0, 0, 0), place(0, 1, 0), place(0, 3, 0), place(0, 0, 1)]
        + [place(0, 2, 0), place(0, 1, 1), place(0, 3, 1), place(0, 2, 1)]
    ).astype(jnp.int32)
    energy_row = jnp.tile(vir_energy, 4).reshape(1, 128)
    core = lax.axis_index("co")
    me = jnp.stack([lax.axis_index("xl") * 32 + place(0, 0, 0), core]).astype(jnp.int32)
    rows = half_rows.reshape(2, 2, 96, AUX)
    given = lax.ppermute(gift(me, screen.T, rows), "co", [(0, 1), (1, 0)])
    meta = slot_map(me, slot_shell)
    most = meta[2, 0]

    def exchange(cap):
        def run(me, screen_t, meta, rows, given, energy_row, vir_coeff):
            packed = pack(cap, me, screen_t, meta, rows, given)
            moved = lax.all_to_all(packed.reshape(64, -1, 128), ("xl",) + GROUP, 0, 0, tiled=True)
            chi, clo = coeff(vir_coeff)
            return transform(cap, meta, moved, energy_row, chi, clo)

        return run

    level = (most > 5).astype(jnp.int32) + (most > 6).astype(jnp.int32)
    sent = lax.switch(
        level, [exchange(5), exchange(6), exchange(8)], me, screen.T, meta, rows, given, energy_row, vir_coeff
    )
    received = lax.all_to_all(sent, GROUP, 0, 0, tiled=True)
    own, energies = unpack(places, received)
    tables = (pair_list.T, occ_energy, energies)
    here, above, below, across = 0, 1, 2, 3

    y1 = take_from(own, "y", 1)
    y3 = take_from(own, "y", -1)
    z1 = take_from(own, "z", 1)
    z3 = take_from(own, "z", -1)
    x0 = take_from(own, "xh", 1)
    y1, y3, z1, z3, x0 = lax.optimization_barrier((y1, y3, z1, z3, x0))
    y2a = take_from(y1[:48], "y", 1)
    y2b = take_from(y3[48:], "y", -1)
    z2 = take_from(z3, "z", -1)
    x1 = take_from(x0, "z", 1)
    x3 = take_from(z3, "xh", 1)
    cols = [own, z1, z3, x0]
    rows, rows_at = [own, y1, y3, y2a, y2b], (here, above, below, across)
    own_acc, near_acc, far_acc = block("gamma_first", tables, rows, rows_at, cols, 4, [], [96, 192, 96])
    z2, x1, x3, own_acc, near_acc, far_acc = lax.optimization_barrier((z2, x1, x3, own_acc, near_acc, far_acc))
    x2a = take_from(z2[:32], "xh", 1)
    x2b = take_from(x1[32:64], "z", 1)
    x2c = take_from(x3[64:], "z", -1)
    own_acc, near_acc, far_acc = block(
        "gamma_next", tables, rows, rows_at, [z2, x1, x3], 8, [own_acc, near_acc, far_acc], [96, 192, 96]
    )
    tail = [x2a, x2b, x2c]
    g2a, g2b = block("gamma_far", tables, [y2a, y2b], (across,), tail, 11, [far_acc], [48, 48])
    up = take_from(g2a, "y", -1)
    down = take_from(g2b, "y", 1)
    g1a, g1b, g3a, g3b = block(
        "gamma_near", tables, [y1, y3], (above, below), tail, 11, [near_acc], [48, 48, 48, 48]
    )
    below_b = take_from(g1b, "y", -1)
    above_a = take_from(g3a, "y", 1)
    (g0,) = block("gamma_own", tables, [own], (here,), tail, 11, [own_acc], [96])
    below_a = take_from(g1a + up, "y", -1)
    above_b = take_from(g3b + down, "y", 1)
    from_below = jnp.concatenate([below_a, below_b], axis=0)
    from_above = jnp.concatenate([above_a, above_b], axis=0)
    return (g0 + from_below + from_above).reshape(3, 32, AUX)


def solution(mesh):
    wide = Mesh(mesh.devices.reshape(2, 2, 4, 4, 2), ALL)
    occ = ("xl", "co")
    in_specs = (P(None, ALL, None), P(None, ALL), P(), P(), P(occ), P(GROUP), P(occ, None))
    out_specs = P(occ, GROUP, None)
    return jax.shard_map(local, mesh=wide, in_specs=in_specs, out_specs=out_specs, check_vma=False)
```

```python
import jax
import jax.numpy as jnp
from jax import lax
from jax.experimental import pallas as pl
from jax.experimental.pallas import tpu as pltpu
from jax.sharding import Mesh, PartitionSpec as P

NVIR = 1024
SHW = 8
NSH = 144
ROWS = NSH * SHW
AUX = 3072
ALL = ("xl", "co", "y", "z", "xh")
GROUP = ("y", "z", "xh")
DEPTH = 1536
VLIM = 60 * 1024 * 1024
f32 = jnp.float32
bf16 = jnp.bfloat16


def params():
    return pltpu.CompilerParams(vmem_limit_bytes=VLIM)


def swap4(v):
    lane = lax.broadcasted_iota(jnp.int32, v[0].shape, 1)
    low = lane < 64
    even = (lane // 32) % 2 == 0
    a0 = jnp.where(low, v[0], pltpu.roll(v[2], 64, 1))
    a2 = jnp.where(low, pltpu.roll(v[0], 64, 1), v[2])
    a1 = jnp.where(low, v[1], pltpu.roll(v[3], 64, 1))
    a3 = jnp.where(low, pltpu.roll(v[1], 64, 1), v[3])
    w0 = jnp.where(even, a0, pltpu.roll(a1, 32, 1))
    w1 = jnp.where(even, pltpu.roll(a0, 96, 1), a1)
    w2 = jnp.where(even, a2, pltpu.roll(a3, 32, 1))
    w3 = jnp.where(even, pltpu.roll(a2, 96, 1), a3)
    return w0, w1, w2, w3


def mix4(v):
    lane = lax.broadcasted_iota(jnp.int32, v[0].shape, 1)
    low = lane < 64
    first = lane < 32
    third = lane < 96
    out = []
    for q in range(4):
        p = [v[(n - q) % 4] for n in range(4)]
        out.append(jnp.where(low, jnp.where(first, p[0], p[1]), jnp.where(third, p[2], p[3])))
    return out


def split(x):
    hi = x.astype(bf16)
    lo = (x - hi.astype(f32)).astype(bf16)
    return hi, lo


def map_kernel(me_ref, row_ref, col_ref, o_ref):
    def parts(g):
        owner = g // 4
        chip = owner // 64 * 32 + owner % 32
        return chip, owner // 32 % 2 * 4 + g % 4

    here, at = parts(lax.broadcasted_iota(jnp.int32, (512, 1), 0))
    there, other = parts(lax.broadcasted_iota(jnp.int32, (1, 512), 1))
    taken = (row_ref[...] >= 0).astype(jnp.int32)
    mates = jnp.where(here == there, taken, 0)
    count = jnp.sum(mates, axis=1, keepdims=True)
    rank = jnp.sum(jnp.where(other < at, mates, 0), axis=1, keepdims=True)
    shell = col_ref[...]
    lane = lax.broadcasted_iota(jnp.int32, (1, 256), 1)
    place = jnp.sum(jnp.where(shell == lane, here * 8 + rank, 0), axis=0, keepdims=True)
    mine = (here == me_ref[0]) & (shell >= 0) & (rank == lane)
    order = jnp.sum(jnp.where(mine, at, 0), axis=0, keepdims=True)
    most = jnp.max(count, axis=0, keepdims=True)
    o_ref[...] = jnp.zeros_like(o_ref)
    o_ref[0:1, :] = place
    o_ref[1:2, :] = order
    o_ref[2:3, :] = jnp.broadcast_to(most, (1, 256))


def slot_map(me, slot_shell):
    vmem = pl.BlockSpec(memory_space=pltpu.VMEM)
    return pl.pallas_call(
        map_kernel,
        in_specs=[pl.BlockSpec(memory_space=pltpu.SMEM), vmem, vmem],
        out_shape=jax.ShapeDtypeStruct((8, 256), jnp.int32),
        compiler_params=pltpu.CompilerParams(vmem_limit_bytes=16 * 1024 * 1024),
        name="slot_map",
    )(me, slot_shell.reshape(1, 512), slot_shell.reshape(512, 1))


def gift_kernel(me_ref, scr_ref, x_ref, o_ref, buf, in_sem, out_sem):
    co = me_ref[1]
    into = []
    for g in range(2):
        for i in range(3):
            n = 3 * g + i
            into.append(pltpu.make_async_copy(x_ref.at[g, 1 - co, 32 * i : 32 * i + 32], buf.at[n], in_sem.at[n]))
            into[n].start()
    out = []
    for g in range(2):
        for i in range(3):
            n = 3 * g + i
            into[n].wait()
            for s in range(4):
                keep = scr_ref[s, (2 * g + 1 - co) * 3 + i].astype(f32)
                buf[n, 8 * s : 8 * s + 8, :] = buf[n, 8 * s : 8 * s + 8, :] * keep
            out.append(pltpu.make_async_copy(buf.at[n], o_ref.at[g, 32 * i : 32 * i + 32], out_sem.at[n]))
            out[n].start()
    for copy in out:
        copy.wait()


def gift(me, screen_t, rows):
    smem = pl.BlockSpec(memory_space=pltpu.SMEM)
    hbm = pl.BlockSpec(memory_space=pl.ANY)
    return pl.pallas_call(
        gift_kernel,
        in_specs=[smem, smem, hbm],
        out_specs=hbm,
        out_shape=jax.ShapeDtypeStruct((2, 96, AUX), f32),
        scratch_shapes=[
            pltpu.VMEM((6, 32, AUX), f32),
            pltpu.SemaphoreType.DMA((6,)),
            pltpu.SemaphoreType.DMA((6,)),
        ],
        compiler_params=pltpu.CompilerParams(vmem_limit_bytes=16 * 1024 * 1024),
        name="gift_rows",
    )(me, screen_t, rows)


def message_rows(cap):
    return 16 * cap + 8 * ((cap + 3) // 4)


def pack_kernel(cap, me_ref, scr_ref, map_ref, x_hbm, y_hbm, o_hbm, x_ref, y_ref, o_ref, in_sem, out_sem):
    co = me_ref[1]

    def into(m):
        at = pl.ds(pl.multiple_of(384 * m, 384), 384)
        return (
            pltpu.make_async_copy(x_hbm.at[:, co, :, at], x_ref.at[m], in_sem.at[0, m]),
            pltpu.make_async_copy(y_hbm.at[:, :, at], y_ref.at[m], in_sem.at[1, m]),
        )

    def out(m):
        return pltpu.make_async_copy(o_ref.at[m], o_hbm.at[:, pl.ds(4 * m, 4)], out_sem.at[m])

    for m in range(8):
        for copy in into(m):
            copy.start()

    def body(m, carry):
        for copy in into(m):
            copy.wait()
        for g in range(2):

            def part(p, i, t):
                place = map_ref[1, p]
                s = place % 4
                at = pl.ds(pl.multiple_of(32 * i + 8 * s, 8), 8)
                cols = slice(128 * t, 128 * t + 128)
                keep = scr_ref[s, (2 * g + co) * 3 + i].astype(f32)
                return jnp.where(place // 4 == co, x_ref[m, g, at, cols] * keep, y_ref[m, g, at, cols])

            for p in range(cap):
                for u in range(2):
                    w = mix4([part(p, *divmod(4 * u + h, 3)) for h in range(4)])
                    for q in range(4):
                        o_ref[m, g, q, 8 * (2 * p + u) : 8 * (2 * p + u) + 8, :] = w[q]
            for four in range((cap + 3) // 4):
                w = swap4([part(min(4 * four + n, cap - 1), 2, 2) for n in range(4)])
                to = 16 * cap + 8 * four
                for q in range(4):
                    o_ref[m, g, q, to : to + 8, :] = w[q]
        out(m).start()
        return carry

    lax.fori_loop(0, 8, body, 0)
    for m in range(8):
        out(m).wait()


def pack(cap, me, screen_t, meta, rows, given):
    size = message_rows(cap)

    def body(*refs):
        pack_kernel(cap, *refs)

    smem = pl.BlockSpec(memory_space=pltpu.SMEM)
    hbm = pl.BlockSpec(memory_space=pl.ANY)
    return pl.pallas_call(
        body,
        in_specs=[smem, smem, smem, hbm, hbm],
        out_specs=hbm,
        out_shape=jax.ShapeDtypeStruct((2, 32, size, 128), f32),
        scratch_shapes=[
            pltpu.VMEM((8, 2, 96, 384), f32),
            pltpu.VMEM((8, 2, 96, 384), f32),
            pltpu.VMEM((8, 2, 4, size, 128), f32),
            pltpu.SemaphoreType.DMA((2, 8)),
            pltpu.SemaphoreType.DMA((8,)),
        ],
        compiler_params=pltpu.CompilerParams(vmem_limit_bytes=24 * 1024 * 1024),
        name=f"pack_rows_{cap}",
    )(me, screen_t, meta, rows, given)


def coeff_kernel(c_ref, hi_ref, lo_ref):
    hi, lo = split(c_ref[...].T)
    hi_ref[...] = hi
    lo_ref[...] = lo


def coeff(vir_coeff):
    return pl.pallas_call(
        coeff_kernel,
        grid=(9,),
        in_specs=[pl.BlockSpec((128, NVIR), lambda k: (k, 0))],
        out_specs=[pl.BlockSpec((NVIR, 128), lambda k: (0, k))] * 2,
        out_shape=[jax.ShapeDtypeStruct((NVIR, ROWS), bf16)] * 2,
        compiler_params=params(),
        name="split_coeff",
    )(vir_coeff)


def transform_kernel(cap, map_ref, r_ref, ve_ref, chi_ref, clo_ref, o_ref, xs):
    @pl.when(pl.program_id(0) == 0)
    def _():
        quarter = lax.broadcasted_iota(jnp.int32, (8, 128), 1) // 32

        def body(h, carry):
            tiles = []
            for e in range(2):
                where = map_ref[0, 2 * h + e]
                chip = where // 8
                rank = where % 8
                t01 = r_ref[chip, pl.ds(pl.multiple_of(rank * 16, 16), 16), :]
                t2 = r_ref[chip, pl.ds(pl.multiple_of(16 * cap + rank // 4 * 8, 8), 8), :]
                t2 = jnp.where(quarter == rank % 4, t2, 0.0)
                tiles.append((t01[:8], t01[8:], t2))
            row = pl.multiple_of(h * 16, 16)
            for n in range(3):
                hi, lo = split(jnp.concatenate([tiles[0][n], tiles[1][n]], axis=0))
                xs[pl.ds(row, 16), 128 * n : 128 * n + 128] = hi
                xs[pl.ds(row, 16), 384 + 128 * n : 512 + 128 * n] = lo
            return carry

        lax.fori_loop(0, NSH // 2, body, 0, unroll=4)

    both = jnp.dot(chi_ref[...], xs[...], preferred_element_type=f32)
    y = both[:, :384] + both[:, 384:]
    y += jnp.dot(clo_ref[...], xs[:, :384], preferred_element_type=f32)
    lane = lax.broadcasted_iota(jnp.int32, (8, 128), 1) // 32
    for k in range(16):
        last = jnp.zeros((8, 128), f32)
        for ag in range(4):
            rows = slice(32 * k + 8 * ag, 32 * k + 8 * ag + 8)
            for u in range(2):
                o_ref[k, 8 * (2 * ag + u) : 8 * (2 * ag + u) + 8, :] = y[rows, 128 * u : 128 * u + 128]
            piece = y[rows, 256:384]
            piece += pltpu.roll(piece, 64, 1)
            piece += pltpu.roll(piece, 32, 1)
            last = jnp.where(lane == ag, piece, last)
        o_ref[k, 64:72, :] = last
        o_ref[k, 72:80, :] = jnp.broadcast_to(ve_ref[...], (8, 128))


def transform(cap, meta, rows, energy_row, chi, clo):
    def body(*refs):
        transform_kernel(cap, *refs)

    return pl.pallas_call(
        body,
        grid=(2,),
        in_specs=[
            pl.BlockSpec(memory_space=pltpu.SMEM),
            pl.BlockSpec((64, message_rows(cap), 128), lambda m: (0, 0, 0)),
            pl.BlockSpec((1, 128), lambda m: (0, 0)),
            pl.BlockSpec((512, ROWS), lambda m: (m, 0)),
            pl.BlockSpec((512, ROWS), lambda m: (m, 0)),
        ],
        out_specs=pl.BlockSpec((16, 80, 128), lambda m: (m, 0, 0)),
        out_shape=jax.ShapeDtypeStruct((32, 80, 128), f32),
        scratch_shapes=[pltpu.VMEM((ROWS, 768), bf16)],
        compiler_params=params(),
        name=f"transform_rows_{cap}",
    )(meta, rows, energy_row, chi, clo)


def unpack_kernel(at_ref, q_ref, f_ref, e_ref):
    for n in range(12):
        e_ref[n : n + 1, :] = q_ref[at_ref[n], 72:73, :]

    def body(m, carry):
        for ag in range(4):
            for u in range(2):
                w = mix4([q_ref[4 * m + q, 8 * (2 * ag + u) : 8 * (2 * ag + u) + 8, :] for q in range(4)])
                for h in range(4):
                    i, t = divmod(4 * u + h, 3)
                    at = pl.multiple_of(384 * m + 128 * t, 128)
                    f_ref[32 * i + 8 * ag : 32 * i + 8 * ag + 8, pl.ds(at, 128)] = w[h]
        w = swap4([q_ref[4 * m + q, 64:72, :] for q in range(4)])
        at = pl.multiple_of(384 * m + 256, 128)
        for ag in range(4):
            f_ref[64 + 8 * ag : 64 + 8 * ag + 8, pl.ds(at, 128)] = w[ag]
        return carry

    lax.fori_loop(0, 8, body, 0)


def unpack(places, received):
    return pl.pallas_call(
        unpack_kernel,
        in_specs=[pl.BlockSpec(memory_space=pltpu.SMEM), pl.BlockSpec(memory_space=pltpu.VMEM)],
        out_shape=[jax.ShapeDtypeStruct((96, AUX), f32), jax.ShapeDtypeStruct((12, 128), f32)],
        compiler_params=params(),
        name="unpack_fitted",
    )(places, received)


def block_kernel(n_a, n_b, n_acc, n_out, shards, row_at, col_at, *refs):
    pairs_ref, oe_ref, e_ref = refs[:3]
    a_refs = refs[3 : 3 + n_a]
    b_refs = refs[3 + n_a : 3 + n_a + n_b]
    acc_refs = refs[3 + n_a + n_b : 3 + n_a + n_b + n_acc]
    outs = refs[3 + n_a + n_b + n_acc : 3 + n_a + n_b + n_acc + n_out]
    a_in, b_in, g_buf, ahi, alo, bst, c_ref, whi, wlo, a_sem, b_sem, acc_sem, out_sem = refs[-13:]
    wide = shards > 1
    width = 384 if wide else 128
    rows_total = ahi.shape[0]

    def into(group, buf, sem):
        copies = []
        row = 0
        for n, ref in enumerate(group):
            h = ref.shape[0]
            copies.append((pltpu.make_async_copy(ref, buf.at[row : row + h], sem.at[n]), row, h))
            row += h
        for copy, _, _ in copies:
            copy.start()
        return copies

    a_copies = into(a_refs, a_in, a_sem)
    b_copies = into(b_refs, b_in, b_sem)
    acc_copies = into(acc_refs, g_buf, acc_sem)
    for copy, row, h in a_copies:
        copy.wait()
        for r in range(row, row + h, 16):
            hi, lo = split(a_in[r : r + 16, :])
            ahi[r : r + 16, :] = hi
            alo[r : r + 16, :] = lo
    for copy, row, h in b_copies:
        copy.wait()
        for r in range(row, row + h, 32):
            shard, j = divmod(r // 32, 3)
            hi, lo = split(b_in[r : r + 32, :])
            to = 128 * j + 32 * shard if wide else 32 * j
            bst[to : to + 32, :] = hi
            bst[width + to : width + to + 32, :] = lo
    blank = [128 * j + 32 * shard for j in range(3) for shard in range(shards, 4)] if wide else [96]
    for to in blank:
        bst[to : to + 32, :] = jnp.zeros((32, AUX), bf16)
        bst[width + to : width + to + 32, :] = jnp.zeros((32, AUX), bf16)
    nt = (((1,), (1,)), ((), ()))

    def coulomb_step(k, carry):
        at = pl.ds(pl.multiple_of(k * DEPTH, DEPTH), DEPTH)
        both = lax.dot_general(ahi[:, at], bst[:, at], nt, preferred_element_type=f32)
        part = both[:, :width] + both[:, width:]
        part += lax.dot_general(alo[:, at], bst[:width, at], nt, preferred_element_type=f32)
        c_ref[...] += part
        return carry

    c_ref[...] = jnp.zeros_like(c_ref)
    lax.fori_loop(0, AUX // DEPTH, coulomb_step, 0)

    group = lax.broadcasted_iota(jnp.int32, (1, 128), 1) // 32
    square = lax.broadcasted_iota(jnp.int32, (32, 128), 0) == lax.broadcasted_iota(jnp.int32, (32, 128), 1)
    chosen = []
    for i in range(3):
        for j in range(3):
            count = jnp.int32(0)
            for n in range(6):
                count += ((pairs_ref[0, n] == i) & (pairs_ref[1, n] == j)).astype(jnp.int32)
            chosen.append(count.astype(f32))
    col = jnp.zeros((1, 128), f32)
    if wide:
        for shard in range(shards):
            col = jnp.where(group == shard, e_ref[col_at + shard : col_at + shard + 1, :], col)
    else:
        piece = e_ref[col_at : col_at + 1, :]
        for j in range(3):
            col = jnp.where(group == j, piece - oe_ref[j], col)
    for d in range(rows_total // 96):
        ea = jnp.sum(jnp.where(square, e_ref[row_at[d] : row_at[d] + 1, :], 0.0), axis=1, keepdims=True)
        for i in range(3):
            rows = slice(96 * d + 32 * i, 96 * d + 32 * i + 32)
            if wide:
                for j in range(3):
                    direct = c_ref[rows, 128 * j : 128 * j + 128]
                    other = c_ref[96 * d + 32 * j : 96 * d + 32 * j + 32, 128 * i : 128 * i + 128]
                    denominator = (oe_ref[i] + oe_ref[j]) - ea - col
                    hi, lo = split(chosen[3 * i + j] * ((2.0 * direct - other) / denominator))
                    whi[rows, 128 * j : 128 * j + 128] = hi
                    whi[rows, 384 + 128 * j : 512 + 128 * j] = hi
                    wlo[rows, 128 * j : 128 * j + 128] = lo
            else:
                direct = c_ref[rows, :]
                other = jnp.zeros((32, 128), f32)
                keep = jnp.zeros((1, 128), f32)
                for j in range(3):
                    moved = c_ref[96 * d + 32 * j : 96 * d + 32 * j + 32, :]
                    if j != i:
                        moved = pltpu.roll(moved, (32 * (j - i)) % 128, 1)
                    other = jnp.where(group == j, moved, other)
                    keep = jnp.where(group == j, chosen[3 * i + j], keep)
                denominator = oe_ref[i] - ea - col
                hi, lo = split(keep * ((2.0 * direct - other) / denominator))
                whi[rows, :128] = hi
                whi[rows, 128:] = hi
                wlo[rows, :] = lo

    for copy, _, _ in acc_copies:
        copy.wait()

    def out_copies(k):
        at = pl.ds(pl.multiple_of(k * 512, 512), 512)
        row = 0
        for n, out in enumerate(outs):
            h = out.shape[0]
            yield pltpu.make_async_copy(g_buf.at[row : row + h, at], out.at[:, at], out_sem.at[k, n])
            row += h

    def gamma_step(k, carry):
        at = pl.ds(pl.multiple_of(k * 512, 512), 512)
        g = jnp.dot(whi[...], bst[:, at], preferred_element_type=f32)
        g += jnp.dot(wlo[...], bst[:width, at], preferred_element_type=f32)
        if n_acc:
            g += g_buf[:, at]
        g_buf[:, at] = g
        for copy in out_copies(k):
            copy.start()
        return carry

    lax.fori_loop(0, AUX // 512, gamma_step, 0)
    for k in range(AUX // 512):
        for copy in out_copies(k):
            copy.wait()


def block(name, tables, a_list, row_at, b_list, col_at, acc_list, out_rows):
    a_list = list(a_list)
    b_list = list(b_list)
    smem = pl.BlockSpec(memory_space=pltpu.SMEM)
    vmem = pl.BlockSpec(memory_space=pltpu.VMEM)
    hbm = pl.BlockSpec(memory_space=pl.ANY)
    rows = sum(a.shape[0] for a in a_list)
    shards = sum(b.shape[0] for b in b_list) // 96
    width = 384 if shards > 1 else 128
    args = list(tables) + a_list + b_list + list(acc_list)
    counts = (len(a_list), len(b_list), len(acc_list), len(out_rows), shards, row_at, col_at)

    def body(*refs):
        block_kernel(*counts, *refs)

    dma = pltpu.SemaphoreType.DMA
    return pl.pallas_call(
        body,
        in_specs=[smem, smem, vmem] + [hbm] * (len(args) - 3),
        out_specs=[hbm] * len(out_rows),
        out_shape=[jax.ShapeDtypeStruct((n, AUX), f32) for n in out_rows],
        scratch_shapes=[
            pltpu.VMEM((rows, AUX), f32),
            pltpu.VMEM((96 * shards, AUX), f32),
            pltpu.VMEM((rows, AUX), f32),
            pltpu.VMEM((rows, AUX), bf16),
            pltpu.VMEM((rows, AUX), bf16),
            pltpu.VMEM((2 * width, AUX), bf16),
            pltpu.VMEM((rows, width), f32),
            pltpu.VMEM((rows, 2 * width), bf16),
            pltpu.VMEM((rows, width), bf16),
            dma((len(a_list),)),
            dma((len(b_list),)),
            dma((max(len(acc_list), 1),)),
            dma((AUX // 512, len(out_rows))),
        ],
        compiler_params=pltpu.CompilerParams(vmem_limit_bytes=36 * 1024 * 1024),
        cost_estimate=pl.CostEstimate(
            flops=2 * rows * width * AUX * 6, transcendentals=0, bytes_accessed=4 * AUX * (2 * rows + 96 * shards)
        ),
        name=name,
    )(*args)


def take_from(x, axis, step):
    n = lax.axis_size(axis)
    return lax.ppermute(x, axis, [(i, (i - step) % n) for i in range(n)])


def local(half_rows, screen, slot_shell, vir_coeff, occ_energy, vir_energy, pair_list):
    y = lax.axis_index("y")
    z = lax.axis_index("z")
    xh = lax.axis_index("xh")

    def place(dy, dz, dx):
        return (y + dy) % 4 * 8 + (z + dz) % 4 * 2 + (xh + dx) % 2

    places = jnp.stack(
        [place(dy, 0, 0) for dy in (0, 1, 3, 2)]
        + [place(0, 0, 0), place(0, 1, 0), place(0, 3, 0), place(0, 0, 1)]
        + [place(0, 2, 0), place(0, 1, 1), place(0, 3, 1), place(0, 2, 1)]
    ).astype(jnp.int32)
    energy_row = jnp.tile(vir_energy, 4).reshape(1, 128)
    core = lax.axis_index("co")
    me = jnp.stack([lax.axis_index("xl") * 32 + place(0, 0, 0), core]).astype(jnp.int32)
    rows = half_rows.reshape(2, 2, 96, AUX)
    given = lax.ppermute(gift(me, screen.T, rows), "co", [(0, 1), (1, 0)])
    meta = slot_map(me, slot_shell)
    most = meta[2, 0]

    def exchange(cap):
        def run(me, screen_t, meta, rows, given, energy_row, vir_coeff):
            packed = pack(cap, me, screen_t, meta, rows, given)
            moved = lax.all_to_all(packed.reshape(64, -1, 128), ("xl",) + GROUP, 0, 0, tiled=True)
            chi, clo = coeff(vir_coeff)
            return transform(cap, meta, moved, energy_row, chi, clo)

        return run

    level = (most > 5).astype(jnp.int32) + (most > 6).astype(jnp.int32)
    sent = lax.switch(
        level, [exchange(5), exchange(6), exchange(8)], me, screen.T, meta, rows, given, energy_row, vir_coeff
    )
    received = lax.all_to_all(sent, GROUP, 0, 0, tiled=True)
    own, energies = unpack(places, received)
    tables = (pair_list.T, occ_energy, energies)
    here, above, below, across = 0, 1, 2, 3

    y1 = take_from(own, "y", 1)
    y3 = take_from(own, "y", -1)
    z1 = take_from(own, "z", 1)
    z3 = take_from(own, "z", -1)
    x0 = take_from(own, "xh", 1)
    y1, y3, z1, z3, x0 = lax.optimization_barrier((y1, y3, z1, z3, x0))
    y2a = take_from(y1[:48], "y", 1)
    y2b = take_from(y3[48:], "y", -1)
    z2 = take_from(z3, "z", -1)
    x1 = take_from(x0, "z", 1)
    x3 = take_from(z3, "xh", 1)
    cols = [own, z1, z3, x0]
    rows, rows_at = [own, y1, y3, y2a, y2b], (here, above, below, across)
    own_acc, near_acc, far_acc = block("gamma_first", tables, rows, rows_at, cols, 4, [], [96, 192, 96])
    z2, x1, x3, own_acc, near_acc, far_acc = lax.optimization_barrier((z2, x1, x3, own_acc, near_acc, far_acc))
    x2a = take_from(z2[:32], "xh", 1)
    x2b = take_from(x1[32:64], "z", 1)
    x2c = take_from(x3[64:], "z", -1)
    own_acc, near_acc, far_acc = block(
        "gamma_next", tables, rows, rows_at, [z2, x1, x3], 8, [own_acc, near_acc, far_acc], [96, 192, 96]
    )
    tail = [x2a, x2b, x2c]
    g2a, g2b = block("gamma_far", tables, [y2a, y2b], (across,), tail, 11, [far_acc], [48, 48])
    up = take_from(g2a, "y", -1)
    down = take_from(g2b, "y", 1)
    g1a, g1b, g3a, g3b = block(
        "gamma_near", tables, [y1, y3], (above, below), tail, 11, [near_acc], [48, 48, 48, 48]
    )
    below_b = take_from(g1b, "y", -1)
    above_a = take_from(g3a, "y", 1)
    (g0,) = block("gamma_own", tables, [own], (here,), tail, 11, [own_acc], [96])
    below_a = take_from(g1a + up, "y", -1)
    above_b = take_from(g3b + down, "y", 1)
    from_below = jnp.concatenate([below_a, below_b], axis=0)
    from_above = jnp.concatenate([above_a, above_b], axis=0)
    return (g0 + from_below + from_above).reshape(3, 32, AUX)


def solution(mesh):
    wide = Mesh(mesh.devices.reshape(2, 2, 4, 4, 2), ALL)
    occ = ("xl", "co")
    in_specs = (P(None, ALL, None), P(None, ALL), P(), P(), P(occ), P(GROUP), P(occ, None))
    out_specs = P(occ, GROUP, None)
    return jax.shard_map(local, mesh=wide, in_specs=in_specs, out_specs=out_specs, check_vma=False)
```

```python
import jax
import jax.numpy as jnp
from jax import lax
from jax.experimental import pallas as pl
from jax.experimental.pallas import tpu as pltpu
from jax.sharding import Mesh, PartitionSpec as P

NVIR = 1024
SHW = 8
NSH = 144
ROWS = NSH * SHW
AUX = 3072
ALL = ("xl", "co", "y", "z", "xh")
GROUP = ("y", "z", "xh")
DEPTH = 1536
VLIM = 60 * 1024 * 1024
f32 = jnp.float32
bf16 = jnp.bfloat16


def params():
    return pltpu.CompilerParams(vmem_limit_bytes=VLIM)


def swap4(v):
    lane = lax.broadcasted_iota(jnp.int32, v[0].shape, 1)
    low = lane < 64
    even = (lane // 32) % 2 == 0
    a0 = jnp.where(low, v[0], pltpu.roll(v[2], 64, 1))
    a2 = jnp.where(low, pltpu.roll(v[0], 64, 1), v[2])
    a1 = jnp.where(low, v[1], pltpu.roll(v[3], 64, 1))
    a3 = jnp.where(low, pltpu.roll(v[1], 64, 1), v[3])
    w0 = jnp.where(even, a0, pltpu.roll(a1, 32, 1))
    w1 = jnp.where(even, pltpu.roll(a0, 96, 1), a1)
    w2 = jnp.where(even, a2, pltpu.roll(a3, 32, 1))
    w3 = jnp.where(even, pltpu.roll(a2, 96, 1), a3)
    return w0, w1, w2, w3


def mix4(v):
    lane = lax.broadcasted_iota(jnp.int32, v[0].shape, 1)
    low = lane < 64
    first = lane < 32
    third = lane < 96
    out = []
    for q in range(4):
        p = [v[(n - q) % 4] for n in range(4)]
        out.append(jnp.where(low, jnp.where(first, p[0], p[1]), jnp.where(third, p[2], p[3])))
    return out


def split(x):
    hi = x.astype(bf16)
    lo = (x - hi.astype(f32)).astype(bf16)
    return hi, lo


def map_kernel(me_ref, row_ref, col_ref, o_ref):
    def parts(g):
        owner = g // 4
        chip = owner // 64 * 32 + owner % 32
        return chip, owner // 32 % 2 * 4 + g % 4

    here, at = parts(lax.broadcasted_iota(jnp.int32, (512, 1), 0))
    there, other = parts(lax.broadcasted_iota(jnp.int32, (1, 512), 1))
    taken = (row_ref[...] >= 0).astype(jnp.int32)
    mates = jnp.where(here == there, taken, 0)
    count = jnp.sum(mates, axis=1, keepdims=True)
    rank = jnp.sum(jnp.where(other < at, mates, 0), axis=1, keepdims=True)
    shell = col_ref[...]
    lane = lax.broadcasted_iota(jnp.int32, (1, 256), 1)
    place = jnp.sum(jnp.where(shell == lane, here * 8 + rank, 0), axis=0, keepdims=True)
    mine = (here == me_ref[0]) & (shell >= 0) & (rank == lane)
    order = jnp.sum(jnp.where(mine, at, 0), axis=0, keepdims=True)
    most = jnp.max(count, axis=0, keepdims=True)
    o_ref[...] = jnp.zeros_like(o_ref)
    o_ref[0:1, :] = place
    o_ref[1:2, :] = order
    o_ref[2:3, :] = jnp.broadcast_to(most, (1, 256))


def slot_map(me, slot_shell):
    vmem = pl.BlockSpec(memory_space=pltpu.VMEM)
    return pl.pallas_call(
        map_kernel,
        in_specs=[pl.BlockSpec(memory_space=pltpu.SMEM), vmem, vmem],
        out_shape=jax.ShapeDtypeStruct((8, 256), jnp.int32),
        compiler_params=pltpu.CompilerParams(vmem_limit_bytes=16 * 1024 * 1024),
        name="slot_map",
    )(me, slot_shell.reshape(1, 512), slot_shell.reshape(512, 1))


def gift_kernel(me_ref, scr_ref, x_ref, o_ref, buf, in_sem, out_sem):
    co = me_ref[1]
    into = []
    for g in range(2):
        for i in range(3):
            n = 3 * g + i
            into.append(pltpu.make_async_copy(x_ref.at[g, 1 - co, 32 * i : 32 * i + 32], buf.at[n], in_sem.at[n]))
            into[n].start()
    out = []
    for g in range(2):
        for i in range(3):
            n = 3 * g + i
            into[n].wait()
            for s in range(4):
                keep = scr_ref[s, (2 * g + 1 - co) * 3 + i].astype(f32)
                buf[n, 8 * s : 8 * s + 8, :] = buf[n, 8 * s : 8 * s + 8, :] * keep
            out.append(pltpu.make_async_copy(buf.at[n], o_ref.at[g, 32 * i : 32 * i + 32], out_sem.at[n]))
            out[n].start()
    for copy in out:
        copy.wait()


def gift(me, screen_t, rows):
    smem = pl.BlockSpec(memory_space=pltpu.SMEM)
    hbm = pl.BlockSpec(memory_space=pl.ANY)
    return pl.pallas_call(
        gift_kernel,
        in_specs=[smem, smem, hbm],
        out_specs=hbm,
        out_shape=jax.ShapeDtypeStruct((2, 96, AUX), f32),
        scratch_shapes=[
            pltpu.VMEM((6, 32, AUX), f32),
            pltpu.SemaphoreType.DMA((6,)),
            pltpu.SemaphoreType.DMA((6,)),
        ],
        compiler_params=pltpu.CompilerParams(vmem_limit_bytes=16 * 1024 * 1024),
        name="gift_rows",
    )(me, screen_t, rows)


def energy_at(cap):
    return 16 * cap + 8 * (cap // 4)


def message_rows(cap):
    return energy_at(cap) + 8


def pack_kernel(cap, me_ref, scr_ref, map_ref, e_ref, x_hbm, y_hbm, o_hbm, x_ref, y_ref, o_ref, in_sem, out_sem):
    co = me_ref[1]

    def into(m):
        at = pl.ds(pl.multiple_of(384 * m, 384), 384)
        return (
            pltpu.make_async_copy(x_hbm.at[:, co, :, at], x_ref.at[m], in_sem.at[0, m]),
            pltpu.make_async_copy(y_hbm.at[:, :, at], y_ref.at[m], in_sem.at[1, m]),
        )

    def out(m):
        return pltpu.make_async_copy(o_ref.at[m], o_hbm.at[:, pl.ds(4 * m, 4)], out_sem.at[m])

    for m in range(8):
        for copy in into(m):
            copy.start()

    def body(m, carry):
        for copy in into(m):
            copy.wait()
        for g in range(2):

            def part(p, i, t):
                place = map_ref[1, p]
                s = place % 4
                at = pl.ds(pl.multiple_of(32 * i + 8 * s, 8), 8)
                cols = slice(128 * t, 128 * t + 128)
                keep = scr_ref[s, (2 * g + co) * 3 + i].astype(f32)
                return jnp.where(place // 4 == co, x_ref[m, g, at, cols] * keep, y_ref[m, g, at, cols])

            for p in range(cap):
                for u in range(2):
                    w = mix4([part(p, *divmod(4 * u + h, 3)) for h in range(4)])
                    for q in range(4):
                        o_ref[m, g, q, 8 * (2 * p + u) : 8 * (2 * p + u) + 8, :] = w[q]
            for four in range((cap + 3) // 4):
                w = swap4([part(min(4 * four + n, cap - 1), 2, 2) for n in range(4)])
                to = 16 * cap + 8 * four
                for q in range(4):
                    o_ref[m, g, q, to : to + 8, :] = jnp.where(tail, energy, w[q]) if to == energy_at(cap) else w[q]
            if cap % 4 == 0:
                for q in range(4):
                    o_ref[m, g, q, energy_at(cap) : energy_at(cap) + 8, :] = energy
        out(m).start()
        return carry

    tail = lax.broadcasted_iota(jnp.int32, (8, 128), 1) >= 96
    energy = jnp.broadcast_to(e_ref[...], (8, 128))
    lax.fori_loop(0, 8, body, 0)
    for m in range(8):
        out(m).wait()


def pack(cap, me, screen_t, meta, energy_row, rows, given):
    size = message_rows(cap)

    def body(*refs):
        pack_kernel(cap, *refs)

    smem = pl.BlockSpec(memory_space=pltpu.SMEM)
    hbm = pl.BlockSpec(memory_space=pl.ANY)
    return pl.pallas_call(
        body,
        in_specs=[smem, smem, smem, pl.BlockSpec(memory_space=pltpu.VMEM), hbm, hbm],
        out_specs=pl.BlockSpec(memory_space=pltpu.HBM),
        out_shape=jax.ShapeDtypeStruct((2, 32, size, 128), f32),
        scratch_shapes=[
            pltpu.VMEM((8, 2, 96, 384), f32),
            pltpu.VMEM((8, 2, 96, 384), f32),
            pltpu.VMEM((8, 2, 4, size, 128), f32),
            pltpu.SemaphoreType.DMA((2, 8)),
            pltpu.SemaphoreType.DMA((8,)),
        ],
        compiler_params=pltpu.CompilerParams(vmem_limit_bytes=60 * 1024 * 1024),
        name=f"pack_rows_{cap}",
    )(me, screen_t, meta, energy_row, rows, given)


def coeff_kernel(c_ref, hi_ref, lo_ref):
    hi, lo = split(c_ref[...].T)
    hi_ref[...] = hi
    lo_ref[...] = lo


def coeff(vir_coeff):
    return pl.pallas_call(
        coeff_kernel,
        grid=(9,),
        in_specs=[pl.BlockSpec((128, NVIR), lambda k: (k, 0))],
        out_specs=[pl.BlockSpec((NVIR, 128), lambda k: (0, k))] * 2,
        out_shape=[jax.ShapeDtypeStruct((NVIR, ROWS), bf16)] * 2,
        compiler_params=params(),
        name="split_coeff",
    )(vir_coeff)


SHARDS = (
    (0, 0, 0), (1, 0, 0), (3, 0, 0), (2, 0, 0),
    (0, 0, 0), (0, 1, 0), (0, 3, 0), (0, 0, 1), (0, 2, 0), (0, 1, 1), (0, 3, 1), (0, 2, 1),
)


def transform_kernel(cap, me_ref, map_ref, r_hbm, chi_ref, clo_ref, o_ref, e_ref, r_ref, xs, sem):
    @pl.when(pl.program_id(0) == 0)
    def _():
        copies = [
            pltpu.make_async_copy(r_hbm.at[16 * n : 16 * n + 16], r_ref.at[16 * n : 16 * n + 16], sem.at[n])
            for n in range(4)
        ]
        for copy in copies:
            copy.start()
        for copy in copies:
            copy.wait()
        blk = me_ref[0] % 32
        y, z, xh = blk // 8, blk // 2 % 4, blk % 2
        lanes = lax.broadcasted_iota(jnp.int32, (1, 128), 1)
        for n, (dy, dz, dx) in enumerate(SHARDS):
            at = (y + dy) % 4 * 8 + (z + dz) % 4 * 2 + (xh + dx) % 2
            line = jnp.where(lanes >= 96, r_ref[at, energy_at(cap) : energy_at(cap) + 1, :], 0.0)
            line += pltpu.roll(line, 64, 1)
            line += pltpu.roll(line, 32, 1)
            e_ref[n : n + 1, :] = line
        quarter = lax.broadcasted_iota(jnp.int32, (8, 128), 1) // 32

        def body(h, carry):
            tiles = []
            for e in range(2):
                where = map_ref[0, 2 * h + e]
                chip = where // 8
                rank = where % 8
                t01 = r_ref[chip, pl.ds(pl.multiple_of(rank * 16, 16), 16), :]
                t2 = r_ref[chip, pl.ds(pl.multiple_of(16 * cap + rank // 4 * 8, 8), 8), :]
                t2 = jnp.where(quarter == rank % 4, t2, 0.0)
                tiles.append((t01[:8], t01[8:], t2))
            row = pl.multiple_of(h * 16, 16)
            for n in range(3):
                hi, lo = split(jnp.concatenate([tiles[0][n], tiles[1][n]], axis=0))
                xs[pl.ds(row, 16), 128 * n : 128 * n + 128] = hi
                xs[pl.ds(row, 16), 384 + 128 * n : 512 + 128 * n] = lo
            return carry

        lax.fori_loop(0, NSH // 2, body, 0, unroll=4)

    both = jnp.dot(chi_ref[...], xs[...], preferred_element_type=f32)
    y = both[:, :384] + both[:, 384:]
    y += jnp.dot(clo_ref[...], xs[:, :384], preferred_element_type=f32)
    lane = lax.broadcasted_iota(jnp.int32, (8, 128), 1) // 32
    for k in range(16):
        last = jnp.zeros((8, 128), f32)
        for ag in range(4):
            rows = slice(32 * k + 8 * ag, 32 * k + 8 * ag + 8)
            for u in range(2):
                o_ref[k, 8 * (2 * ag + u) : 8 * (2 * ag + u) + 8, :] = y[rows, 128 * u : 128 * u + 128]
            piece = y[rows, 256:384]
            piece += pltpu.roll(piece, 64, 1)
            piece += pltpu.roll(piece, 32, 1)
            last = jnp.where(lane == ag, piece, last)
        o_ref[k, 64:72, :] = last


def transform(cap, me, meta, rows, chi, clo):
    def body(*refs):
        transform_kernel(cap, *refs)

    return pl.pallas_call(
        body,
        grid=(2,),
        in_specs=[
            pl.BlockSpec(memory_space=pltpu.SMEM),
            pl.BlockSpec(memory_space=pltpu.SMEM),
            pl.BlockSpec(memory_space=pl.ANY),
            pl.BlockSpec((512, ROWS), lambda m: (m, 0)),
            pl.BlockSpec((512, ROWS), lambda m: (m, 0)),
        ],
        out_specs=[pl.BlockSpec((16, 72, 128), lambda m: (m, 0, 0)), pl.BlockSpec((12, 128), lambda m: (0, 0))],
        out_shape=[jax.ShapeDtypeStruct((32, 72, 128), f32), jax.ShapeDtypeStruct((12, 128), f32)],
        scratch_shapes=[
            pltpu.VMEM((64, message_rows(cap), 128), f32),
            pltpu.VMEM((ROWS, 768), bf16),
            pltpu.SemaphoreType.DMA((4,)),
        ],
        compiler_params=pltpu.CompilerParams(vmem_limit_bytes=36 * 1024 * 1024),
        name=f"transform_rows_{cap}",
    )(me, meta, rows, chi, clo)


def unpack_kernel(q_hbm, f_hbm, q_ref, f_ref, in_sem, out_sem):
    def into(m):
        at = pl.ds(4 * m, 4)
        return pltpu.make_async_copy(q_hbm.at[at], q_ref.at[at], in_sem.at[m])

    def out(m):
        at = pl.ds(pl.multiple_of(384 * m, 384), 384)
        return pltpu.make_async_copy(f_ref.at[:, at], f_hbm.at[:, at], out_sem.at[m])

    for m in range(8):
        into(m).start()

    def body(m, carry):
        into(m).wait()
        for ag in range(4):
            for u in range(2):
                w = mix4([q_ref[4 * m + q, 8 * (2 * ag + u) : 8 * (2 * ag + u) + 8, :] for q in range(4)])
                for h in range(4):
                    i, t = divmod(4 * u + h, 3)
                    at = pl.multiple_of(384 * m + 128 * t, 128)
                    f_ref[32 * i + 8 * ag : 32 * i + 8 * ag + 8, pl.ds(at, 128)] = w[h]
        w = swap4([q_ref[4 * m + q, 64:72, :] for q in range(4)])
        at = pl.multiple_of(384 * m + 256, 128)
        for ag in range(4):
            f_ref[64 + 8 * ag : 64 + 8 * ag + 8, pl.ds(at, 128)] = w[ag]
        out(m).start()
        return carry

    lax.fori_loop(0, 8, body, 0)
    for m in range(8):
        out(m).wait()


def unpack(received):
    hbm = pl.BlockSpec(memory_space=pl.ANY)
    return pl.pallas_call(
        unpack_kernel,
        in_specs=[hbm],
        out_specs=hbm,
        out_shape=jax.ShapeDtypeStruct((96, AUX), f32),
        scratch_shapes=[
            pltpu.VMEM((32, 72, 128), f32),
            pltpu.VMEM((96, AUX), f32),
            pltpu.SemaphoreType.DMA((8,)),
            pltpu.SemaphoreType.DMA((8,)),
        ],
        compiler_params=pltpu.CompilerParams(vmem_limit_bytes=16 * 1024 * 1024),
        name="unpack_fitted",
    )(received)


def block_kernel(n_a, n_b, n_acc, n_out, shards, row_at, col_at, *refs):
    pairs_ref, oe_ref, e_ref = refs[:3]
    a_refs = refs[3 : 3 + n_a]
    b_refs = refs[3 + n_a : 3 + n_a + n_b]
    acc_refs = refs[3 + n_a + n_b : 3 + n_a + n_b + n_acc]
    outs = refs[3 + n_a + n_b + n_acc : 3 + n_a + n_b + n_acc + n_out]
    a_in, b_in, g_buf, ahi, alo, bst, c_ref, whi, wlo, a_sem, b_sem, acc_sem, out_sem = refs[-13:]
    wide = shards > 1
    width = 384 if wide else 128
    rows_total = ahi.shape[0]

    def into(group, buf, sem):
        copies = []
        row = 0
        for n, ref in enumerate(group):
            h = ref.shape[0]
            copies.append((pltpu.make_async_copy(ref, buf.at[row : row + h], sem.at[n]), row, h))
            row += h
        for copy, _, _ in copies:
            copy.start()
        return copies

    a_copies = into(a_refs, a_in, a_sem)
    b_copies = into(b_refs, b_in, b_sem)
    acc_copies = into(acc_refs, g_buf, acc_sem)
    for copy, row, h in a_copies:
        copy.wait()
        for r in range(row, row + h, 16):
            hi, lo = split(a_in[r : r + 16, :])
            ahi[r : r + 16, :] = hi
            alo[r : r + 16, :] = lo
    for copy, row, h in b_copies:
        copy.wait()
        for r in range(row, row + h, 32):
            shard, j = divmod(r // 32, 3)
            hi, lo = split(b_in[r : r + 32, :])
            to = 128 * j + 32 * shard if wide else 32 * j
            bst[to : to + 32, :] = hi
            bst[width + to : width + to + 32, :] = lo
    blank = [128 * j + 32 * shard for j in range(3) for shard in range(shards, 4)] if wide else [96]
    for to in blank:
        bst[to : to + 32, :] = jnp.zeros((32, AUX), bf16)
        bst[width + to : width + to + 32, :] = jnp.zeros((32, AUX), bf16)
    nt = (((1,), (1,)), ((), ()))

    def coulomb_step(k, carry):
        at = pl.ds(pl.multiple_of(k * DEPTH, DEPTH), DEPTH)
        both = lax.dot_general(ahi[:, at], bst[:, at], nt, preferred_element_type=f32)
        part = both[:, :width] + both[:, width:]
        part += lax.dot_general(alo[:, at], bst[:width, at], nt, preferred_element_type=f32)
        c_ref[...] += part
        return carry

    c_ref[...] = jnp.zeros_like(c_ref)
    lax.fori_loop(0, AUX // DEPTH, coulomb_step, 0)

    group = lax.broadcasted_iota(jnp.int32, (1, 128), 1) // 32
    square = lax.broadcasted_iota(jnp.int32, (32, 128), 0) == lax.broadcasted_iota(jnp.int32, (32, 128), 1)
    chosen = []
    for i in range(3):
        for j in range(3):
            count = jnp.int32(0)
            for n in range(6):
                count += ((pairs_ref[0, n] == i) & (pairs_ref[1, n] == j)).astype(jnp.int32)
            chosen.append(count.astype(f32))
    col = jnp.zeros((1, 128), f32)
    if wide:
        for shard in range(shards):
            col = jnp.where(group == shard, e_ref[col_at + shard : col_at + shard + 1, :], col)
    else:
        piece = e_ref[col_at : col_at + 1, :]
        for j in range(3):
            col = jnp.where(group == j, piece - oe_ref[j], col)
    for d in range(rows_total // 96):
        ea = jnp.sum(jnp.where(square, e_ref[row_at[d] : row_at[d] + 1, :], 0.0), axis=1, keepdims=True)
        for i in range(3):
            rows = slice(96 * d + 32 * i, 96 * d + 32 * i + 32)
            if wide:
                for j in range(3):
                    direct = c_ref[rows, 128 * j : 128 * j + 128]
                    other = c_ref[96 * d + 32 * j : 96 * d + 32 * j + 32, 128 * i : 128 * i + 128]
                    denominator = (oe_ref[i] + oe_ref[j]) - ea - col
                    hi, lo = split(chosen[3 * i + j] * ((2.0 * direct - other) / denominator))
                    whi[rows, 128 * j : 128 * j + 128] = hi
                    whi[rows, 384 + 128 * j : 512 + 128 * j] = hi
                    wlo[rows, 128 * j : 128 * j + 128] = lo
            else:
                direct = c_ref[rows, :]
                other = jnp.zeros((32, 128), f32)
                keep = jnp.zeros((1, 128), f32)
                for j in range(3):
                    moved = c_ref[96 * d + 32 * j : 96 * d + 32 * j + 32, :]
                    if j != i:
                        moved = pltpu.roll(moved, (32 * (j - i)) % 128, 1)
                    other = jnp.where(group == j, moved, other)
                    keep = jnp.where(group == j, chosen[3 * i + j], keep)
                denominator = oe_ref[i] - ea - col
                hi, lo = split(keep * ((2.0 * direct - other) / denominator))
                whi[rows, :128] = hi
                whi[rows, 128:] = hi
                wlo[rows, :] = lo

    for copy, _, _ in acc_copies:
        copy.wait()

    def out_copies(k):
        at = pl.ds(pl.multiple_of(k * 512, 512), 512)
        row = 0
        for n, out in enumerate(outs):
            h = out.shape[0]
            yield pltpu.make_async_copy(g_buf.at[row : row + h, at], out.at[:, at], out_sem.at[k, n])
            row += h

    def gamma_step(k, carry):
        at = pl.ds(pl.multiple_of(k * 512, 512), 512)
        g = jnp.dot(whi[...], bst[:, at], preferred_element_type=f32)
        g += jnp.dot(wlo[...], bst[:width, at], preferred_element_type=f32)
        if n_acc:
            g += g_buf[:, at]
        g_buf[:, at] = g
        for copy in out_copies(k):
            copy.start()
        return carry

    lax.fori_loop(0, AUX // 512, gamma_step, 0)
    for k in range(AUX // 512):
        for copy in out_copies(k):
            copy.wait()


def block(name, tables, a_list, row_at, b_list, col_at, acc_list, out_rows):
    a_list = list(a_list)
    b_list = list(b_list)
    smem = pl.BlockSpec(memory_space=pltpu.SMEM)
    vmem = pl.BlockSpec(memory_space=pltpu.VMEM)
    hbm = pl.BlockSpec(memory_space=pl.ANY)
    rows = sum(a.shape[0] for a in a_list)
    shards = sum(b.shape[0] for b in b_list) // 96
    width = 384 if shards > 1 else 128
    args = list(tables) + a_list + b_list + list(acc_list)
    counts = (len(a_list), len(b_list), len(acc_list), len(out_rows), shards, row_at, col_at)

    def body(*refs):
        block_kernel(*counts, *refs)

    dma = pltpu.SemaphoreType.DMA
    return pl.pallas_call(
        body,
        in_specs=[smem, smem, vmem] + [hbm] * (len(args) - 3),
        out_specs=[hbm] * len(out_rows),
        out_shape=[jax.ShapeDtypeStruct((n, AUX), f32) for n in out_rows],
        scratch_shapes=[
            pltpu.VMEM((rows, AUX), f32),
            pltpu.VMEM((96 * shards, AUX), f32),
            pltpu.VMEM((rows, AUX), f32),
            pltpu.VMEM((rows, AUX), bf16),
            pltpu.VMEM((rows, AUX), bf16),
            pltpu.VMEM((2 * width, AUX), bf16),
            pltpu.VMEM((rows, width), f32),
            pltpu.VMEM((rows, 2 * width), bf16),
            pltpu.VMEM((rows, width), bf16),
            dma((len(a_list),)),
            dma((len(b_list),)),
            dma((max(len(acc_list), 1),)),
            dma((AUX // 512, len(out_rows))),
        ],
        compiler_params=pltpu.CompilerParams(vmem_limit_bytes=36 * 1024 * 1024),
        cost_estimate=pl.CostEstimate(
            flops=2 * rows * width * AUX * 6, transcendentals=0, bytes_accessed=4 * AUX * (2 * rows + 96 * shards)
        ),
        name=name,
    )(*args)


def take_from(x, axis, step):
    n = lax.axis_size(axis)
    return lax.ppermute(x, axis, [(i, (i - step) % n) for i in range(n)])


def local(half_rows, screen, slot_shell, vir_coeff, occ_energy, vir_energy, pair_list):
    y = lax.axis_index("y")
    z = lax.axis_index("z")
    xh = lax.axis_index("xh")

    energy_row = jnp.tile(vir_energy, 4).reshape(1, 128)
    core = lax.axis_index("co")
    me = jnp.stack([lax.axis_index("xl") * 32 + y * 8 + z * 2 + xh, core]).astype(jnp.int32)
    rows = half_rows.reshape(2, 2, 96, AUX)
    given = lax.ppermute(gift(me, screen.T, rows), "co", [(0, 1), (1, 0)])
    meta = slot_map(me, slot_shell)
    most = meta[2, 0]

    def exchange(cap):
        def run(me, screen_t, meta, rows, given, energy_row, vir_coeff):
            packed = pack(cap, me, screen_t, meta, energy_row, rows, given)
            moved = lax.all_to_all(packed.reshape(64, -1, 128), ("xl",) + GROUP, 0, 0, tiled=True)
            chi, clo = coeff(vir_coeff)
            return transform(cap, me, meta, moved, chi, clo)

        return run

    level = (most > 5).astype(jnp.int32) + (most > 6).astype(jnp.int32)
    sent, energies = lax.switch(
        level, [exchange(5), exchange(6), exchange(8)], me, screen.T, meta, rows, given, energy_row, vir_coeff
    )
    received = lax.all_to_all(sent, GROUP, 0, 0, tiled=True)
    own = unpack(received)
    tables = (pair_list.T, occ_energy, energies)
    here, above, below, across = 0, 1, 2, 3

    y1 = take_from(own, "y", 1)
    y3 = take_from(own, "y", -1)
    z1 = take_from(own, "z", 1)
    z3 = take_from(own, "z", -1)
    x0 = take_from(own, "xh", 1)
    y1, y3, z1, z3, x0 = lax.optimization_barrier((y1, y3, z1, z3, x0))
    y2a = take_from(y1[:48], "y", 1)
    y2b = take_from(y3[48:], "y", -1)
    z2 = take_from(z3, "z", -1)
    x1 = take_from(x0, "z", 1)
    x3 = take_from(z3, "xh", 1)
    cols = [own, z1, z3, x0]
    rows, rows_at = [own, y1, y3, y2a, y2b], (here, above, below, across)
    own_acc, near_acc, far_acc = block("gamma_first", tables, rows, rows_at, cols, 4, [], [96, 192, 96])
    z2, x1, x3, own_acc, near_acc, far_acc = lax.optimization_barrier((z2, x1, x3, own_acc, near_acc, far_acc))
    x2a = take_from(z2[:32], "xh", 1)
    x2b = take_from(x1[32:64], "z", 1)
    x2c = take_from(x3[64:], "z", -1)
    own_acc, near_acc, far_acc = block(
        "gamma_next", tables, rows, rows_at, [z2, x1, x3], 8, [own_acc, near_acc, far_acc], [96, 192, 96]
    )
    tail = [x2a, x2b, x2c]
    g2a, g2b = block("gamma_far", tables, [y2a, y2b], (across,), tail, 11, [far_acc], [48, 48])
    up = take_from(g2a, "y", -1)
    down = take_from(g2b, "y", 1)
    g1a, g1b, g3a, g3b = block(
        "gamma_near", tables, [y1, y3], (above, below), tail, 11, [near_acc], [48, 48, 48, 48]
    )
    below_b = take_from(g1b, "y", -1)
    above_a = take_from(g3a, "y", 1)
    (g0,) = block("gamma_own", tables, [own], (here,), tail, 11, [own_acc], [96])
    below_a = take_from(g1a + up, "y", -1)
    above_b = take_from(g3b + down, "y", 1)
    from_below = jnp.concatenate([below_a, below_b], axis=0)
    from_above = jnp.concatenate([above_a, above_b], axis=0)
    return (g0 + from_below + from_above).reshape(3, 32, AUX)


def solution(mesh):
    wide = Mesh(mesh.devices.reshape(2, 2, 4, 4, 2), ALL)
    occ = ("xl", "co")
    in_specs = (P(None, ALL, None), P(None, ALL), P(), P(), P(occ), P(GROUP), P(occ, None))
    out_specs = P(occ, GROUP, None)
    return jax.shard_map(local, mesh=wide, in_specs=in_specs, out_specs=out_specs, check_vma=False)
```

```python
import jax
import jax.numpy as jnp
from jax import lax
from jax.experimental import pallas as pl
from jax.experimental.pallas import tpu as pltpu
from jax.sharding import Mesh, PartitionSpec as P

NVIR = 1024
SHW = 8
NSH = 144
ROWS = NSH * SHW
AUX = 3072
ALL = ("xl", "co", "y", "z", "xh")
GROUP = ("y", "z", "xh")
DEPTH = 1536
VLIM = 60 * 1024 * 1024
f32 = jnp.float32
bf16 = jnp.bfloat16


def params():
    return pltpu.CompilerParams(vmem_limit_bytes=VLIM)


def swap4(v):
    lane = lax.broadcasted_iota(jnp.int32, v[0].shape, 1)
    low = lane < 64
    even = (lane // 32) % 2 == 0
    a0 = jnp.where(low, v[0], pltpu.roll(v[2], 64, 1))
    a2 = jnp.where(low, pltpu.roll(v[0], 64, 1), v[2])
    a1 = jnp.where(low, v[1], pltpu.roll(v[3], 64, 1))
    a3 = jnp.where(low, pltpu.roll(v[1], 64, 1), v[3])
    w0 = jnp.where(even, a0, pltpu.roll(a1, 32, 1))
    w1 = jnp.where(even, pltpu.roll(a0, 96, 1), a1)
    w2 = jnp.where(even, a2, pltpu.roll(a3, 32, 1))
    w3 = jnp.where(even, pltpu.roll(a2, 96, 1), a3)
    return w0, w1, w2, w3


def mix4(v):
    lane = lax.broadcasted_iota(jnp.int32, v[0].shape, 1)
    low = lane < 64
    first = lane < 32
    third = lane < 96
    out = []
    for q in range(4):
        p = [v[(n - q) % 4] for n in range(4)]
        out.append(jnp.where(low, jnp.where(first, p[0], p[1]), jnp.where(third, p[2], p[3])))
    return out


def split(x):
    hi = x.astype(bf16)
    lo = (x - hi.astype(f32)).astype(bf16)
    return hi, lo


def map_kernel(me_ref, row_ref, col_ref, o_ref):
    def parts(g):
        owner = g // 4
        chip = owner // 64 * 32 + owner % 32
        return chip, owner // 32 % 2 * 4 + g % 4

    here, at = parts(lax.broadcasted_iota(jnp.int32, (512, 1), 0))
    there, other = parts(lax.broadcasted_iota(jnp.int32, (1, 512), 1))
    taken = (row_ref[...] >= 0).astype(jnp.int32)
    mates = jnp.where(here == there, taken, 0)
    count = jnp.sum(mates, axis=1, keepdims=True)
    rank = jnp.sum(jnp.where(other < at, mates, 0), axis=1, keepdims=True)
    shell = col_ref[...]
    lane = lax.broadcasted_iota(jnp.int32, (1, 256), 1)
    place = jnp.sum(jnp.where(shell == lane, here * 8 + rank, 0), axis=0, keepdims=True)
    mine = (here == me_ref[0]) & (shell >= 0) & (rank == lane)
    order = jnp.sum(jnp.where(mine, at, 0), axis=0, keepdims=True)
    most = jnp.max(count, axis=0, keepdims=True)
    o_ref[...] = jnp.zeros_like(o_ref)
    o_ref[0:1, :] = place
    o_ref[1:2, :] = order
    o_ref[2:3, :] = jnp.broadcast_to(most, (1, 256))


def slot_map(me, slot_shell):
    vmem = pl.BlockSpec(memory_space=pltpu.VMEM)
    return pl.pallas_call(
        map_kernel,
        in_specs=[pl.BlockSpec(memory_space=pltpu.SMEM), vmem, vmem],
        out_shape=jax.ShapeDtypeStruct((8, 256), jnp.int32),
        compiler_params=pltpu.CompilerParams(vmem_limit_bytes=16 * 1024 * 1024),
        name="slot_map",
    )(me, slot_shell.reshape(1, 512), slot_shell.reshape(512, 1))


def gift_kernel(me_ref, scr_ref, x_ref, o_ref, buf, in_sem, out_sem):
    co = me_ref[1]
    into = []
    for g in range(2):
        for i in range(3):
            n = 3 * g + i
            into.append(pltpu.make_async_copy(x_ref.at[g, 1 - co, 32 * i : 32 * i + 32], buf.at[n], in_sem.at[n]))
            into[n].start()
    out = []
    for g in range(2):
        for i in range(3):
            n = 3 * g + i
            into[n].wait()
            for s in range(4):
                keep = scr_ref[s, (2 * g + 1 - co) * 3 + i].astype(f32)
                buf[n, 8 * s : 8 * s + 8, :] = buf[n, 8 * s : 8 * s + 8, :] * keep
            out.append(pltpu.make_async_copy(buf.at[n], o_ref.at[g, 32 * i : 32 * i + 32], out_sem.at[n]))
            out[n].start()
    for copy in out:
        copy.wait()


def gift(me, screen_t, rows):
    smem = pl.BlockSpec(memory_space=pltpu.SMEM)
    hbm = pl.BlockSpec(memory_space=pl.ANY)
    return pl.pallas_call(
        gift_kernel,
        in_specs=[smem, smem, hbm],
        out_specs=hbm,
        out_shape=jax.ShapeDtypeStruct((2, 96, AUX), f32),
        scratch_shapes=[
            pltpu.VMEM((6, 32, AUX), f32),
            pltpu.SemaphoreType.DMA((6,)),
            pltpu.SemaphoreType.DMA((6,)),
        ],
        compiler_params=pltpu.CompilerParams(vmem_limit_bytes=16 * 1024 * 1024),
        name="gift_rows",
    )(me, screen_t, rows)


def energy_at(cap):
    return 16 * cap + 8 * (cap // 4)


def message_rows(cap):
    return energy_at(cap) + 8


def pack_kernel(cap, me_ref, scr_ref, map_ref, e_ref, x_hbm, y_hbm, o_hbm, x_ref, y_ref, o_ref, in_sem, out_sem):
    co = me_ref[1]

    def into(m):
        at = pl.ds(pl.multiple_of(384 * m, 384), 384)
        return (
            pltpu.make_async_copy(x_hbm.at[:, co, :, at], x_ref.at[m], in_sem.at[0, m]),
            pltpu.make_async_copy(y_hbm.at[:, :, at], y_ref.at[m], in_sem.at[1, m]),
        )

    def out(m):
        return pltpu.make_async_copy(o_ref.at[m], o_hbm.at[:, pl.ds(4 * m, 4)], out_sem.at[m])

    for m in range(8):
        for copy in into(m):
            copy.start()

    def body(m, carry):
        for copy in into(m):
            copy.wait()
        for g in range(2):

            def part(p, i, t):
                place = map_ref[1, p]
                s = place % 4
                at = pl.ds(pl.multiple_of(32 * i + 8 * s, 8), 8)
                cols = slice(128 * t, 128 * t + 128)
                keep = scr_ref[s, (2 * g + co) * 3 + i].astype(f32)
                return jnp.where(place // 4 == co, x_ref[m, g, at, cols] * keep, y_ref[m, g, at, cols])

            for p in range(cap):
                for u in range(2):
                    w = mix4([part(p, *divmod(4 * u + h, 3)) for h in range(4)])
                    for q in range(4):
                        o_ref[m, g, q, 8 * (2 * p + u) : 8 * (2 * p + u) + 8, :] = w[q]
            for four in range((cap + 3) // 4):
                w = swap4([part(min(4 * four + n, cap - 1), 2, 2) for n in range(4)])
                to = 16 * cap + 8 * four
                for q in range(4):
                    o_ref[m, g, q, to : to + 8, :] = jnp.where(tail, energy, w[q]) if to == energy_at(cap) else w[q]
            if cap % 4 == 0:
                for q in range(4):
                    o_ref[m, g, q, energy_at(cap) : energy_at(cap) + 8, :] = energy
        out(m).start()
        return carry

    tail = lax.broadcasted_iota(jnp.int32, (8, 128), 1) >= 96
    energy = jnp.broadcast_to(e_ref[...], (8, 128))
    lax.fori_loop(0, 8, body, 0)
    for m in range(8):
        out(m).wait()


def pack(cap, me, screen_t, meta, energy_row, rows, given):
    size = message_rows(cap)

    def body(*refs):
        pack_kernel(cap, *refs)

    smem = pl.BlockSpec(memory_space=pltpu.SMEM)
    hbm = pl.BlockSpec(memory_space=pl.ANY)
    return pl.pallas_call(
        body,
        in_specs=[smem, smem, smem, pl.BlockSpec(memory_space=pltpu.VMEM), hbm, hbm],
        out_specs=pl.BlockSpec(memory_space=pltpu.HBM),
        out_shape=jax.ShapeDtypeStruct((2, 32, size, 128), f32),
        scratch_shapes=[
            pltpu.VMEM((8, 2, 96, 384), f32),
            pltpu.VMEM((8, 2, 96, 384), f32),
            pltpu.VMEM((8, 2, 4, size, 128), f32),
            pltpu.SemaphoreType.DMA((2, 8)),
            pltpu.SemaphoreType.DMA((8,)),
        ],
        compiler_params=pltpu.CompilerParams(vmem_limit_bytes=60 * 1024 * 1024),
        name=f"pack_rows_{cap}",
    )(me, screen_t, meta, energy_row, rows, given)


def coeff_kernel(c_ref, hi_ref, lo_ref):
    hi, lo = split(c_ref[...].T)
    hi_ref[...] = hi
    lo_ref[...] = lo


def coeff(vir_coeff):
    return pl.pallas_call(
        coeff_kernel,
        grid=(9,),
        in_specs=[pl.BlockSpec((128, NVIR), lambda k: (k, 0))],
        out_specs=[pl.BlockSpec((NVIR, 128), lambda k: (0, k))] * 2,
        out_shape=[jax.ShapeDtypeStruct((NVIR, ROWS), bf16)] * 2,
        compiler_params=pltpu.CompilerParams(vmem_limit_bytes=64500 * 1024),
        name="split_coeff",
    )(vir_coeff)


SHARDS = (
    (0, 0, 0), (1, 0, 0), (3, 0, 0), (2, 0, 0),
    (0, 0, 0), (0, 1, 0), (0, 3, 0), (0, 0, 1), (0, 2, 0), (0, 1, 1), (0, 3, 1), (0, 2, 1),
)


def transform_kernel(cap, me_ref, map_ref, r_hbm, hi_hbm, lo_hbm, o_ref, e_ref, r_ref, chi_ref, clo_ref, xs, sem, c_sem):
    step = pl.program_id(0)

    def halves(m):
        at = pl.ds(pl.multiple_of(512 * m, 512), 512)
        return (
            pltpu.make_async_copy(hi_hbm.at[at], chi_ref.at[at], c_sem.at[0, m]),
            pltpu.make_async_copy(lo_hbm.at[at], clo_ref.at[at], c_sem.at[1, m]),
        )

    @pl.when(pl.program_id(0) == 0)
    def _():
        copies = [
            pltpu.make_async_copy(r_hbm.at[16 * n : 16 * n + 16], r_ref.at[16 * n : 16 * n + 16], sem.at[n])
            for n in range(4)
        ]
        for copy in copies:
            copy.start()
        for m in range(2):
            for copy in halves(m):
                copy.start()
        for copy in copies:
            copy.wait()
        blk = me_ref[0] % 32
        y, z, xh = blk // 8, blk // 2 % 4, blk % 2
        lanes = lax.broadcasted_iota(jnp.int32, (1, 128), 1)
        for n, (dy, dz, dx) in enumerate(SHARDS):
            at = (y + dy) % 4 * 8 + (z + dz) % 4 * 2 + (xh + dx) % 2
            line = jnp.where(lanes >= 96, r_ref[at, energy_at(cap) : energy_at(cap) + 1, :], 0.0)
            line += pltpu.roll(line, 64, 1)
            line += pltpu.roll(line, 32, 1)
            e_ref[n : n + 1, :] = line
        quarter = lax.broadcasted_iota(jnp.int32, (8, 128), 1) // 32

        def body(h, carry):
            tiles = []
            for e in range(2):
                where = map_ref[0, 2 * h + e]
                chip = where // 8
                rank = where % 8
                t01 = r_ref[chip, pl.ds(pl.multiple_of(rank * 16, 16), 16), :]
                t2 = r_ref[chip, pl.ds(pl.multiple_of(16 * cap + rank // 4 * 8, 8), 8), :]
                t2 = jnp.where(quarter == rank % 4, t2, 0.0)
                tiles.append((t01[:8], t01[8:], t2))
            row = pl.multiple_of(h * 16, 16)
            for n in range(3):
                hi, lo = split(jnp.concatenate([tiles[0][n], tiles[1][n]], axis=0))
                xs[pl.ds(row, 16), 128 * n : 128 * n + 128] = hi
                xs[pl.ds(row, 16), 384 + 128 * n : 512 + 128 * n] = lo
            return carry

        lax.fori_loop(0, NSH // 2, body, 0, unroll=4)

    for copy in halves(step):
        copy.wait()
    mine = pl.ds(pl.multiple_of(512 * step, 512), 512)
    both = jnp.dot(chi_ref[mine, :], xs[...], preferred_element_type=f32)
    y = both[:, :384] + both[:, 384:]
    y += jnp.dot(clo_ref[mine, :], xs[:, :384], preferred_element_type=f32)
    lane = lax.broadcasted_iota(jnp.int32, (8, 128), 1) // 32
    for k in range(16):
        last = jnp.zeros((8, 128), f32)
        for ag in range(4):
            rows = slice(32 * k + 8 * ag, 32 * k + 8 * ag + 8)
            for u in range(2):
                o_ref[k, 8 * (2 * ag + u) : 8 * (2 * ag + u) + 8, :] = y[rows, 128 * u : 128 * u + 128]
            piece = y[rows, 256:384]
            piece += pltpu.roll(piece, 64, 1)
            piece += pltpu.roll(piece, 32, 1)
            last = jnp.where(lane == ag, piece, last)
        o_ref[k, 64:72, :] = last


def transform(cap, me, meta, rows, chi, clo):
    def body(*refs):
        transform_kernel(cap, *refs)

    return pl.pallas_call(
        body,
        grid=(2,),
        in_specs=[
            pl.BlockSpec(memory_space=pltpu.SMEM),
            pl.BlockSpec(memory_space=pltpu.SMEM),
            pl.BlockSpec(memory_space=pl.ANY),
            pl.BlockSpec(memory_space=pl.ANY),
            pl.BlockSpec(memory_space=pl.ANY),
        ],
        out_specs=[pl.BlockSpec((16, 72, 128), lambda m: (m, 0, 0)), pl.BlockSpec((12, 128), lambda m: (0, 0))],
        out_shape=[jax.ShapeDtypeStruct((32, 72, 128), f32), jax.ShapeDtypeStruct((12, 128), f32)],
        scratch_shapes=[
            pltpu.VMEM((64, message_rows(cap), 128), f32),
            pltpu.VMEM((NVIR, ROWS), bf16),
            pltpu.VMEM((NVIR, ROWS), bf16),
            pltpu.VMEM((ROWS, 768), bf16),
            pltpu.SemaphoreType.DMA((4,)),
            pltpu.SemaphoreType.DMA((2, 2)),
        ],
        compiler_params=pltpu.CompilerParams(vmem_limit_bytes=60 * 1024 * 1024),
        name=f"transform_rows_{cap}",
    )(me, meta, rows, chi, clo)


def unpack_kernel(q_hbm, f_hbm, q_ref, f_ref, in_sem, out_sem):
    def into(m):
        at = pl.ds(4 * m, 4)
        return pltpu.make_async_copy(q_hbm.at[at], q_ref.at[at], in_sem.at[m])

    def out(m):
        at = pl.ds(pl.multiple_of(384 * m, 384), 384)
        return pltpu.make_async_copy(f_ref.at[:, at], f_hbm.at[:, at], out_sem.at[m])

    for m in range(8):
        into(m).start()

    def body(m, carry):
        into(m).wait()
        for ag in range(4):
            for u in range(2):
                w = mix4([q_ref[4 * m + q, 8 * (2 * ag + u) : 8 * (2 * ag + u) + 8, :] for q in range(4)])
                for h in range(4):
                    i, t = divmod(4 * u + h, 3)
                    at = pl.multiple_of(384 * m + 128 * t, 128)
                    f_ref[32 * i + 8 * ag : 32 * i + 8 * ag + 8, pl.ds(at, 128)] = w[h]
        w = swap4([q_ref[4 * m + q, 64:72, :] for q in range(4)])
        at = pl.multiple_of(384 * m + 256, 128)
        for ag in range(4):
            f_ref[64 + 8 * ag : 64 + 8 * ag + 8, pl.ds(at, 128)] = w[ag]
        out(m).start()
        return carry

    lax.fori_loop(0, 8, body, 0)
    for m in range(8):
        out(m).wait()


def unpack(received):
    hbm = pl.BlockSpec(memory_space=pl.ANY)
    return pl.pallas_call(
        unpack_kernel,
        in_specs=[hbm],
        out_specs=hbm,
        out_shape=jax.ShapeDtypeStruct((96, AUX), f32),
        scratch_shapes=[
            pltpu.VMEM((32, 72, 128), f32),
            pltpu.VMEM((96, AUX), f32),
            pltpu.SemaphoreType.DMA((8,)),
            pltpu.SemaphoreType.DMA((8,)),
        ],
        compiler_params=pltpu.CompilerParams(vmem_limit_bytes=16 * 1024 * 1024),
        name="unpack_fitted",
    )(received)


def block_kernel(n_a, n_b, n_acc, n_out, shards, row_at, col_at, *refs):
    pairs_ref, oe_ref, e_ref = refs[:3]
    a_refs = refs[3 : 3 + n_a]
    b_refs = refs[3 + n_a : 3 + n_a + n_b]
    acc_refs = refs[3 + n_a + n_b : 3 + n_a + n_b + n_acc]
    outs = refs[3 + n_a + n_b + n_acc : 3 + n_a + n_b + n_acc + n_out]
    a_in, b_in, g_buf, ahi, alo, bst, c_ref, whi, wlo, a_sem, b_sem, acc_sem, out_sem = refs[-13:]
    wide = shards > 1
    width = 384 if wide else 128
    rows_total = ahi.shape[0]

    def into(group, buf, sem):
        copies = []
        row = 0
        for n, ref in enumerate(group):
            h = ref.shape[0]
            copies.append((pltpu.make_async_copy(ref, buf.at[row : row + h], sem.at[n]), row, h))
            row += h
        for copy, _, _ in copies:
            copy.start()
        return copies

    a_copies = into(a_refs, a_in, a_sem)
    b_copies = into(b_refs, b_in, b_sem)
    acc_copies = into(acc_refs, g_buf, acc_sem)
    for copy, row, h in a_copies:
        copy.wait()
        for r in range(row, row + h, 16):
            hi, lo = split(a_in[r : r + 16, :])
            ahi[r : r + 16, :] = hi
            alo[r : r + 16, :] = lo
    for copy, row, h in b_copies:
        copy.wait()
        for r in range(row, row + h, 32):
            shard, j = divmod(r // 32, 3)
            hi, lo = split(b_in[r : r + 32, :])
            to = 128 * j + 32 * shard if wide else 32 * j
            bst[to : to + 32, :] = hi
            bst[width + to : width + to + 32, :] = lo
    blank = [128 * j + 32 * shard for j in range(3) for shard in range(shards, 4)] if wide else [96]
    for to in blank:
        bst[to : to + 32, :] = jnp.zeros((32, AUX), bf16)
        bst[width + to : width + to + 32, :] = jnp.zeros((32, AUX), bf16)
    nt = (((1,), (1,)), ((), ()))

    def coulomb_step(k, carry):
        at = pl.ds(pl.multiple_of(k * DEPTH, DEPTH), DEPTH)
        both = lax.dot_general(ahi[:, at], bst[:, at], nt, preferred_element_type=f32)
        part = both[:, :width] + both[:, width:]
        part += lax.dot_general(alo[:, at], bst[:width, at], nt, preferred_element_type=f32)
        c_ref[...] += part
        return carry

    c_ref[...] = jnp.zeros_like(c_ref)
    lax.fori_loop(0, AUX // DEPTH, coulomb_step, 0)

    group = lax.broadcasted_iota(jnp.int32, (1, 128), 1) // 32
    square = lax.broadcasted_iota(jnp.int32, (32, 128), 0) == lax.broadcasted_iota(jnp.int32, (32, 128), 1)
    chosen = []
    for i in range(3):
        for j in range(3):
            count = jnp.int32(0)
            for n in range(6):
                count += ((pairs_ref[0, n] == i) & (pairs_ref[1, n] == j)).astype(jnp.int32)
            chosen.append(count.astype(f32))
    col = jnp.zeros((1, 128), f32)
    if wide:
        for shard in range(shards):
            col = jnp.where(group == shard, e_ref[col_at + shard : col_at + shard + 1, :], col)
    else:
        piece = e_ref[col_at : col_at + 1, :]
        for j in range(3):
            col = jnp.where(group == j, piece - oe_ref[j], col)
    for d in range(rows_total // 96):
        ea = jnp.sum(jnp.where(square, e_ref[row_at[d] : row_at[d] + 1, :], 0.0), axis=1, keepdims=True)
        for i in range(3):
            rows = slice(96 * d + 32 * i, 96 * d + 32 * i + 32)
            if wide:
                for j in range(3):
                    direct = c_ref[rows, 128 * j : 128 * j + 128]
                    other = c_ref[96 * d + 32 * j : 96 * d + 32 * j + 32, 128 * i : 128 * i + 128]
                    denominator = (oe_ref[i] + oe_ref[j]) - ea - col
                    hi, lo = split(chosen[3 * i + j] * ((2.0 * direct - other) / denominator))
                    whi[rows, 128 * j : 128 * j + 128] = hi
                    whi[rows, 384 + 128 * j : 512 + 128 * j] = hi
                    wlo[rows, 128 * j : 128 * j + 128] = lo
            else:
                direct = c_ref[rows, :]
                other = jnp.zeros((32, 128), f32)
                keep = jnp.zeros((1, 128), f32)
                for j in range(3):
                    moved = c_ref[96 * d + 32 * j : 96 * d + 32 * j + 32, :]
                    if j != i:
                        moved = pltpu.roll(moved, (32 * (j - i)) % 128, 1)
                    other = jnp.where(group == j, moved, other)
                    keep = jnp.where(group == j, chosen[3 * i + j], keep)
                denominator = oe_ref[i] - ea - col
                hi, lo = split(keep * ((2.0 * direct - other) / denominator))
                whi[rows, :128] = hi
                whi[rows, 128:] = hi
                wlo[rows, :] = lo

    for copy, _, _ in acc_copies:
        copy.wait()

    def out_copies(k):
        at = pl.ds(pl.multiple_of(k * 512, 512), 512)
        row = 0
        for n, out in enumerate(outs):
            h = out.shape[0]
            yield pltpu.make_async_copy(g_buf.at[row : row + h, at], out.at[:, at], out_sem.at[k, n])
            row += h

    def gamma_step(k, carry):
        at = pl.ds(pl.multiple_of(k * 512, 512), 512)
        g = jnp.dot(whi[...], bst[:, at], preferred_element_type=f32)
        g += jnp.dot(wlo[...], bst[:width, at], preferred_element_type=f32)
        if n_acc:
            g += g_buf[:, at]
        g_buf[:, at] = g
        for copy in out_copies(k):
            copy.start()
        return carry

    lax.fori_loop(0, AUX // 512, gamma_step, 0)
    for k in range(AUX // 512):
        for copy in out_copies(k):
            copy.wait()


def block(name, tables, a_list, row_at, b_list, col_at, acc_list, out_rows):
    a_list = list(a_list)
    b_list = list(b_list)
    smem = pl.BlockSpec(memory_space=pltpu.SMEM)
    vmem = pl.BlockSpec(memory_space=pltpu.VMEM)
    hbm = pl.BlockSpec(memory_space=pl.ANY)
    rows = sum(a.shape[0] for a in a_list)
    shards = sum(b.shape[0] for b in b_list) // 96
    width = 384 if shards > 1 else 128
    args = list(tables) + a_list + b_list + list(acc_list)
    counts = (len(a_list), len(b_list), len(acc_list), len(out_rows), shards, row_at, col_at)

    def body(*refs):
        block_kernel(*counts, *refs)

    dma = pltpu.SemaphoreType.DMA
    return pl.pallas_call(
        body,
        in_specs=[smem, smem, vmem] + [hbm] * (len(args) - 3),
        out_specs=[hbm] * len(out_rows),
        out_shape=[jax.ShapeDtypeStruct((n, AUX), f32) for n in out_rows],
        scratch_shapes=[
            pltpu.VMEM((rows, AUX), f32),
            pltpu.VMEM((96 * shards, AUX), f32),
            pltpu.VMEM((rows, AUX), f32),
            pltpu.VMEM((rows, AUX), bf16),
            pltpu.VMEM((rows, AUX), bf16),
            pltpu.VMEM((2 * width, AUX), bf16),
            pltpu.VMEM((rows, width), f32),
            pltpu.VMEM((rows, 2 * width), bf16),
            pltpu.VMEM((rows, width), bf16),
            dma((len(a_list),)),
            dma((len(b_list),)),
            dma((max(len(acc_list), 1),)),
            dma((AUX // 512, len(out_rows))),
        ],
        compiler_params=pltpu.CompilerParams(vmem_limit_bytes=36 * 1024 * 1024),
        cost_estimate=pl.CostEstimate(
            flops=2 * rows * width * AUX * 6, transcendentals=0, bytes_accessed=4 * AUX * (2 * rows + 96 * shards)
        ),
        name=name,
    )(*args)


def take_from(x, axis, step):
    n = lax.axis_size(axis)
    return lax.ppermute(x, axis, [(i, (i - step) % n) for i in range(n)])


def local(half_rows, screen, slot_shell, vir_coeff, occ_energy, vir_energy, pair_list):
    y = lax.axis_index("y")
    z = lax.axis_index("z")
    xh = lax.axis_index("xh")

    energy_row = jnp.tile(vir_energy, 4).reshape(1, 128)
    core = lax.axis_index("co")
    me = jnp.stack([lax.axis_index("xl") * 32 + y * 8 + z * 2 + xh, core]).astype(jnp.int32)
    rows = half_rows.reshape(2, 2, 96, AUX)
    given = lax.ppermute(gift(me, screen.T, rows), "co", [(0, 1), (1, 0)])
    meta = slot_map(me, slot_shell)
    most = meta[2, 0]

    def exchange(cap):
        def run(me, screen_t, meta, rows, given, energy_row, vir_coeff):
            packed = pack(cap, me, screen_t, meta, energy_row, rows, given)
            moved = lax.all_to_all(packed.reshape(64, -1, 128), ("xl",) + GROUP, 0, 0, tiled=True)
            chi, clo = coeff(vir_coeff)
            return transform(cap, me, meta, moved, chi, clo)

        return run

    level = (most > 5).astype(jnp.int32) + (most > 6).astype(jnp.int32)
    sent, energies = lax.switch(
        level, [exchange(5), exchange(6), exchange(8)], me, screen.T, meta, rows, given, energy_row, vir_coeff
    )
    received = lax.all_to_all(sent, GROUP, 0, 0, tiled=True)
    own = unpack(received)
    tables = (pair_list.T, occ_energy, energies)
    here, above, below, across = 0, 1, 2, 3

    y1 = take_from(own, "y", 1)
    y3 = take_from(own, "y", -1)
    z1 = take_from(own, "z", 1)
    z3 = take_from(own, "z", -1)
    x0 = take_from(own, "xh", 1)
    y1, y3, z1, z3, x0 = lax.optimization_barrier((y1, y3, z1, z3, x0))
    y2a = take_from(y1[:48], "y", 1)
    y2b = take_from(y3[48:], "y", -1)
    z2 = take_from(z3, "z", -1)
    x1 = take_from(x0, "z", 1)
    x3 = take_from(z3, "xh", 1)
    cols = [own, z1, z3, x0]
    rows, rows_at = [own, y1, y3, y2a, y2b], (here, above, below, across)
    own_acc, near_acc, far_acc = block("gamma_first", tables, rows, rows_at, cols, 4, [], [96, 192, 96])
    z2, x1, x3, own_acc, near_acc, far_acc = lax.optimization_barrier((z2, x1, x3, own_acc, near_acc, far_acc))
    x2a = take_from(z2[:32], "xh", 1)
    x2b = take_from(x1[32:64], "z", 1)
    x2c = take_from(x3[64:], "z", -1)
    own_acc, near_acc, far_acc = block(
        "gamma_next", tables, rows, rows_at, [z2, x1, x3], 8, [own_acc, near_acc, far_acc], [96, 192, 96]
    )
    tail = [x2a, x2b, x2c]
    g2a, g2b = block("gamma_far", tables, [y2a, y2b], (across,), tail, 11, [far_acc], [48, 48])
    up = take_from(g2a, "y", -1)
    down = take_from(g2b, "y", 1)
    g1a, g1b, g3a, g3b = block(
        "gamma_near", tables, [y1, y3], (above, below), tail, 11, [near_acc], [48, 48, 48, 48]
    )
    below_b = take_from(g1b, "y", -1)
    above_a = take_from(g3a, "y", 1)
    (g0,) = block("gamma_own", tables, [own], (here,), tail, 11, [own_acc], [96])
    below_a = take_from(g1a + up, "y", -1)
    above_b = take_from(g3b + down, "y", 1)
    from_below = jnp.concatenate([below_a, below_b], axis=0)
    from_above = jnp.concatenate([above_a, above_b], axis=0)
    return (g0 + from_below + from_above).reshape(3, 32, AUX)


def solution(mesh):
    wide = Mesh(mesh.devices.reshape(2, 2, 4, 4, 2), ALL)
    occ = ("xl", "co")
    in_specs = (P(None, ALL, None), P(None, ALL), P(), P(), P(occ), P(GROUP), P(occ, None))
    out_specs = P(occ, GROUP, None)
    return jax.shard_map(local, mesh=wide, in_specs=in_specs, out_specs=out_specs, check_vma=False)
```
